256 devices in a mesh: tm: 16 (over z, x_hi), space: 16 (over x_lo, y, core).
Axes of the slice: x: 4 (x_hi: 2, x_lo: 2; x = x_hi * 2 + x_lo), y: 4, z: 8, core: 2. Of those that a mesh axis runs over, the one named last changes fastest.
Arguments:
- starts: float32 [16, 16384, 128], P('tm', 'space'), may hold values from -7.5 to 9
- region: int32 [1024, 8], P('space'), may hold values from 0 to 7
- viscosity: float32 [8], replicated, may hold values from 0.5 to 1.5
- heat_source: float32 [16384, 128], P('space'), may hold values from -2.1 to 2.1
- fine_line: float32 [128, 128], replicated, may hold values from 0 to 0.5
- coarse_line: float32 [128, 128], replicated, may hold values from 0 to 0.5
Outputs:
- ends: float32 [16, 16384, 128], P('tm', 'space')
- next_starts: float32 [16, 16384, 128], P('tm', 'space')
The draws below stay inside these ranges and needn't reach their ends.
All inputs are finite; a program needn't handle non-finite values.
Results may differ from the reference program's by a relative error of at most 0.00012.
Values sent between devices are 32-bit elements; how exact they have to be, the bound alone decides.
No kernel may reach another device: no remote copies, remote signals or barrier semaphores. Data moves between devices by JAX's collectives and lax.ppermute only.
A program may use at most 64 MiB of HBM per device.

```python
import math
import jax
import jax.numpy as jnp
from jax import lax

NY = 128
CELL_BLOCK = 16
REGIONS = 8
STEPS = 8
GROUPS = 16
NX = 16384


band_length = 2.0


band_total = 2.0 / (math.exp(1.0 / band_length) - 1.0)


def line_matrix(key, diag_lo, diag_hi, spread):
    key_off, key_diag = jax.random.split(key)
    weights = jax.random.uniform(key_off, (NY, NY), jnp.float32, 0.5, 1.0)
    rows = jnp.arange(NY, dtype=jnp.float32)[:, None]
    cols = jnp.arange(NY, dtype=jnp.float32)[None, :]
    envelope = jnp.exp(-jnp.abs(rows - cols) / band_length)
    off = weights * envelope * (spread / band_total)
    diag = jax.random.uniform(key_diag, (NY,), jnp.float32, diag_lo, diag_hi)
    unit = jnp.eye(NY, dtype=jnp.float32)
    return off * (1.0 - unit) + unit * diag[None, :]


def draw_fine_line(key, part):
    return line_matrix(jax.random.fold_in(key, 11), 0.4, 0.46, 0.74)


def draw_coarse_line(key, part):
    return line_matrix(jax.random.fold_in(key, 23), 0.36, 0.42, 0.66)


def draw_starts(key, part):
    key_rough, key_amp, key_phx, key_phy = jax.random.split(jax.random.fold_in(key, 37), 4)
    key_plug, key_grain = jax.random.split(jax.random.fold_in(key, 53))
    rough = jnp.clip(jax.random.normal(key_rough, (GROUPS, NX, NY), jnp.float32), -6.0, 6.0)
    along = jnp.arange(NX, dtype=jnp.float32)[None, :, None] * (2.0 * jnp.pi / NX)
    cross = jnp.arange(NY, dtype=jnp.float32)[None, None, :] * (jnp.pi / NY)
    phase_x = jax.random.uniform(key_phx, (GROUPS, 1, 1), jnp.float32, 0.0, 2.0 * jnp.pi)
    phase_y = jax.random.uniform(key_phy, (GROUPS, 1, 1), jnp.float32, 0.0, 2.0 * jnp.pi)
    parity = jnp.arange(NX, dtype=jnp.int32) % 2
    sign = (1 - 2 * parity).astype(jnp.float32)[None, :, None]
    plug_height = jax.random.uniform(key_plug, (GROUPS, NX, 1), jnp.float32, 1.5, 3.0)
    grain = jax.random.uniform(key_grain, (GROUPS, NX, NY), jnp.float32, 0.7, 1.3)
    plugs = sign * plug_height * grain
    amplitude = jax.random.uniform(key_amp, (GROUPS, 1, 1), jnp.float32, -1.0, 1.0)
    smooth = amplitude * jnp.cos(along + phase_x) * (1.0 + 0.3 * jnp.cos(cross + phase_y))
    return jnp.clip(rough + smooth + plugs, -7.5, 9.0)


def draw_heat_source(key, part):
    key_rough, key_amp, key_phx, key_phy = jax.random.split(jax.random.fold_in(key, 41), 4)
    rough = jnp.clip(0.5 * jax.random.normal(key_rough, (NX, NY), jnp.float32), -2.0, 2.0)
    along = jnp.arange(NX, dtype=jnp.float32)[:, None] * (2.0 * jnp.pi / NX)
    cross = jnp.arange(NY, dtype=jnp.float32)[None, :] * (jnp.pi / NY)
    phase_x = jax.random.uniform(key_phx, (), jnp.float32, 0.0, 2.0 * jnp.pi)
    phase_y = jax.random.uniform(key_phy, (), jnp.float32, 0.0, 2.0 * jnp.pi)
    amplitude = jax.random.uniform(key_amp, (), jnp.float32, -0.02, 0.02)
    smooth = amplitude * jnp.cos(along + phase_x) * (1.0 + 0.3 * jnp.cos(cross + phase_y))
    return rough + smooth


def touch_ends(entries, key, least, top_value):
    longest = entries.shape.index(max(entries.shape))
    spots = []
    for shift in (0, 1):
        where = [jax.random.randint(jax.random.fold_in(key, axis), (), 0, length) for axis, length in enumerate(entries.shape)]
        where[longest] = (where[longest] + shift) % entries.shape[longest]
        spots.append(tuple(where))
    return entries.at[spots[0]].set(least).at[spots[1]].set(top_value)


def setup_inputs(seed: int = 0) -> dict:
    streams_of = jax.random.split(jax.random.key(seed), 7)
    return {
        "starts": draw_starts(jax.random.fold_in(streams_of[6], 71), 0),
        "region": touch_ends(jax.random.randint(streams_of[1], (NX // CELL_BLOCK, NY // CELL_BLOCK), 0, REGIONS), jax.random.fold_in(streams_of[1], 1), 0, REGIONS - 1).astype(jnp.int32),
        "viscosity": jnp.clip(jnp.exp(jax.random.uniform(streams_of[2], (REGIONS,), jnp.float32, math.log(0.5), math.log(1.5))), 0.5, 1.5),
        "heat_source": draw_heat_source(jax.random.fold_in(streams_of[6], 71), 0),
        "fine_line": draw_fine_line(jax.random.fold_in(streams_of[6], 71), 0),
        "coarse_line": draw_coarse_line(jax.random.fold_in(streams_of[6], 71), 0),
    }


FINE_C = 0.3
FINE_R = 0.2
COARSE_C = 0.5
COARSE_R = 0.12
COARSE_Q = 3.0
SOFTEN = 0.5


def viscous(base, field):
    return base / (1.0 + SOFTEN * field * field)


def explicit(u_pad, m_pad, source, courant, ratio):
    middle = u_pad[1:-1]
    below = u_pad[:-2]
    above = u_pad[2:]
    face_up = 0.5 * (m_pad[1:-1] + m_pad[2:])
    face_down = 0.5 * (m_pad[1:-1] + m_pad[:-2])
    return middle - courant * (middle - below) + ratio * (face_up * (above - middle) - face_down * (middle - below)) + source


def across(field, line):
    return jnp.dot(field, line.T, precision=lax.Precision.HIGHEST, preferred_element_type=jnp.float32)


def pad_rows(field):
    return jnp.pad(field, ((1, 1), (0, 0)))


def advance(state, base_pad, source, courant, ratio, line):
    u_pad = pad_rows(state)
    first = across(explicit(u_pad, viscous(base_pad, u_pad), source, courant, ratio), line)
    w_pad = pad_rows(first)
    return across(explicit(u_pad, viscous(base_pad, 0.5 * (u_pad + w_pad)), source, courant, ratio), line)


def base_field(region, viscosity):
    picks = (region[:, :, None] == jnp.arange(REGIONS, dtype=jnp.int32)).astype(jnp.float32)
    blocks = jnp.sum(picks * viscosity[None, None, :], axis=2)
    rows, cols = blocks.shape
    spread = jnp.broadcast_to(blocks[:, None, :, None], (rows, CELL_BLOCK, cols, CELL_BLOCK))
    return spread.reshape(rows * CELL_BLOCK, cols * CELL_BLOCK)


def reference(starts, region, viscosity, heat_source, fine_line, coarse_line):
    base_pad = pad_rows(base_field(region, viscosity))
    coarse_source = COARSE_Q * heat_source

    def fine(start):
        state = start
        for step in range(STEPS):
            state = advance(state, base_pad, heat_source, FINE_C, FINE_R, fine_line)
        return state

    def coarse(state):
        return advance(state, base_pad, coarse_source, COARSE_C, COARSE_R, coarse_line)

    fine_ends = lax.map(fine, starts)
    coarse_starts = lax.map(coarse, starts)
    jumps = fine_ends - coarse_starts

    def sweep(previous, jump):
        value = coarse(previous) + jump
        return value, value

    final, later = lax.scan(sweep, fine_ends[0], jumps[1:])
    ends = jnp.concatenate([fine_ends[:1], later], axis=0)
    next_starts = jnp.concatenate([starts[:1], ends[:-1]], axis=0)
    return ends, next_starts
```

```python
import functools

import jax
import jax.numpy as jnp
from jax import lax
from jax.experimental import pallas as pl
from jax.experimental.pallas import tpu as pltpu
from jax.sharding import PartitionSpec as P

NY = 128
CELL_BLOCK = 16
REGIONS = 8
STEPS = 8

FINE_C = 0.3
FINE_R = 0.2
COARSE_C = 0.5
COARSE_R = 0.12
COARSE_Q = 3.0

HALO = 48
HALO_BLOCKS = HALO // CELL_BLOCK
PACK = 2 * HALO + 8
WINDOW = 128
MARGIN = 28
BACK = WINDOW - 2 * MARGIN
VMEM_LIMIT = 48 * 1024 * 1024


def from_left(tile):
    return pltpu.roll(tile, 1, 0)


def from_right(tile):
    return pltpu.roll(tile, 7, 0)


def halves(x):
    high = x.astype(jnp.bfloat16)
    low = (x - high.astype(jnp.float32)).astype(jnp.bfloat16)
    return high, low


def line_operand(line_ref):
    high, low = halves(line_ref[...].T)
    top = jnp.concatenate([high, low], axis=1)
    return jnp.concatenate([top, top], axis=0)


def product(pairs, rhs_ref):
    left = jnp.concatenate([jnp.concatenate(halves(e), axis=1) for e in pairs], axis=0)
    both = jnp.dot(left, rhs_ref[...], preferred_element_type=jnp.float32)
    return both[:, :NY] + both[:, NY:]


def flux_pass(tiles, chunk, viscosity_of, slope_of, base_of, walls, rhs_ref, store):
    pairs = tiles // 2
    m = viscosity_of(0)
    last = m if pairs == 1 else viscosity_of(pairs - 1)
    wrapped = from_right(m[:8])
    edge = (last[8:] + wrapped) * slope_of(pairs - 1)[8:]
    before = from_left(edge)
    done, first = [], 0
    for i in range(pairs):
        if i + 1 < pairs:
            following = last if i + 1 == pairs - 1 else viscosity_of(i + 1)
            above = jnp.concatenate([m[8:], following[:8]], axis=0)
        else:
            following = None
            above = jnp.concatenate([m[8:], wrapped], axis=0)
        flux = (m + above) * slope_of(i)
        under = jnp.concatenate([before, flux[:8]], axis=0)
        e = base_of(i) + (flux - under)
        for tile, mask in walls:
            if tile // 2 == i:
                ones = jnp.ones_like(mask)
                both = [mask, ones] if tile % 2 == 0 else [ones, mask]
                e = e * jnp.concatenate(both, axis=0)
        before = flux[8:]
        m = following
        done.append(e)
        if len(done) * 2 == chunk or i + 1 == pairs:
            store(first, len(done) * 16, product(done, rhs_ref))
            done, first = [], 16 * (i + 1)


def advance(tiles, chunk, u_ref, base_ref, heat_ref, still_ref, slope_ref, w_ref, rhs_ref, courant, ratio, weight, walls, store):
    pairs = tiles // 2

    def rows(i):
        return slice(16 * i, 16 * i + 16)

    def viscosity_first(i):
        u = u_ref[rows(i), :]
        return base_ref[rows(i), :] / (2.0 + u * u)

    def viscosity_second(i):
        u = 0.5 * (u_ref[rows(i), :] + w_ref[rows(i), :])
        return base_ref[rows(i), :] / (2.0 + u * u)

    right = from_right(u_ref[0:8, :])
    difference = {}

    def step_up(i):
        if i not in difference:
            u = u_ref[rows(i), :]
            if i + 1 < pairs:
                above = u_ref[16 * i + 8 : 16 * i + 24, :]
            else:
                above = jnp.concatenate([u[8:], right], axis=0)
            difference[i] = above - u
        return difference[i]

    def slope_first(i):
        slope = ratio * step_up(i)
        slope_ref[rows(i), :] = slope
        return slope

    def still_first(i):
        up = courant * step_up(i)
        if i == 0:
            prior = from_left(courant * step_up(pairs - 1)[8:])
        else:
            prior = courant * step_up(i - 1)[8:]
        heat = heat_ref[rows(i), :]
        if weight != 1.0:
            heat = weight * heat
        still = (u_ref[rows(i), :] + heat) - jnp.concatenate([prior, up[:8]], axis=0)
        still_ref[rows(i), :] = still
        return still

    def store_first(start, count, value):
        w_ref[start : start + count, :] = value

    flux_pass(tiles, chunk, viscosity_first, slope_first, still_first, walls, rhs_ref, store_first)
    flux_pass(
        tiles,
        chunk,
        viscosity_second,
        lambda i: slope_ref[rows(i), :],
        lambda i: still_ref[rows(i), :],
        walls,
        rhs_ref,
        store,
    )


def wall(at_wall, sublane):
    row = lax.broadcasted_iota(jnp.int32, (8, NY), 0)
    return jnp.where((row == sublane) & at_wall, 0.0, 1.0)


def whole(shape):
    return pl.BlockSpec(shape, lambda: (0,) * len(shape))


ANYWHERE = pl.BlockSpec(memory_space=pl.ANY)


def pack_kernel(viscosity_ref, region_ref, start_ref, heat_ref, head_ref, tail_ref, blocks_ref, sems):
    slab = start_ref.shape[0]
    copies = [
        pltpu.make_async_copy(start_ref.at[pl.ds(0, HALO)], head_ref.at[pl.ds(0, HALO)], sems.at[0]),
        pltpu.make_async_copy(heat_ref.at[pl.ds(0, HALO)], head_ref.at[pl.ds(HALO, HALO)], sems.at[1]),
        pltpu.make_async_copy(start_ref.at[pl.ds(slab - HALO, HALO)], tail_ref.at[pl.ds(0, HALO)], sems.at[2]),
        pltpu.make_async_copy(heat_ref.at[pl.ds(slab - HALO, HALO)], tail_ref.at[pl.ds(HALO, HALO)], sems.at[3]),
    ]
    for copy in copies:
        copy.start()
    region = region_ref[...]
    count = region.shape[0]
    lane = lax.broadcasted_iota(jnp.int32, (count, NY), 1) // CELL_BLOCK
    spread = jnp.zeros((count, NY), jnp.int32)
    for col in range(NY // CELL_BLOCK):
        spread = jnp.where(lane == col, region[:, col : col + 1], spread)
    blocks = jnp.zeros((count, NY), jnp.float32)
    for value in range(REGIONS):
        blocks = jnp.where(spread == value, viscosity_ref[value], blocks)
    blocks_ref[...] = blocks
    head_ref[2 * HALO :, :] = blocks[:8]
    tail_ref[2 * HALO :, :] = blocks[count - 8 :]
    for copy in copies:
        copy.wait()


def pack(viscosity, region, start, heat):
    count = region.shape[0]
    return pl.pallas_call(
        pack_kernel,
        out_shape=(
            jax.ShapeDtypeStruct((PACK, NY), jnp.float32),
            jax.ShapeDtypeStruct((PACK, NY), jnp.float32),
            jax.ShapeDtypeStruct((count, NY), jnp.float32),
        ),
        in_specs=[pl.BlockSpec(memory_space=pltpu.SMEM), whole(region.shape), ANYWHERE, ANYWHERE],
        out_specs=(whole((PACK, NY)), whole((PACK, NY)), whole((count, NY))),
        scratch_shapes=[pltpu.SemaphoreType.DMA((4,))],
        name="pack",
    )(viscosity, region, start, heat)


def fine_kernel(
    ends,
    low_ref,
    high_ref,
    start_ref,
    heat_ref,
    blocks_ref,
    fine_ref,
    coarse_ref,
    windows_ref,
    own_ref,
    base_ref,
    source_ref,
    base_window_ref,
    source_window_ref,
    plain_u,
    plain_q,
    plain_m,
    u_ref,
    still_ref,
    slope_ref,
    w_ref,
    fine_rhs,
    coarse_rhs,
    sems,
    window_sems,
):
    space, group = lax.axis_index("space"), lax.axis_index("tm")
    slab = start_ref.shape[0]
    total = slab + 2 * HALO
    tiles = total // 8
    copies = []
    for n, (plain, part, middle) in enumerate(((plain_u, 0, start_ref), (plain_q, HALO, heat_ref))):
        copies += [
            pltpu.make_async_copy(low_ref.at[pl.ds(part, HALO)], plain.at[pl.ds(0, HALO)], sems.at[3 * n]),
            pltpu.make_async_copy(middle, plain.at[pl.ds(HALO, slab)], sems.at[3 * n + 1]),
            pltpu.make_async_copy(high_ref.at[pl.ds(part, HALO)], plain.at[pl.ds(HALO + slab, HALO)], sems.at[3 * n + 2]),
        ]
    blocks_low = pltpu.make_async_copy(low_ref.at[pl.ds(2 * HALO, 8)], still_ref.at[pl.ds(0, 8)], sems.at[6])
    blocks_high = pltpu.make_async_copy(high_ref.at[pl.ds(2 * HALO, 8)], still_ref.at[pl.ds(8, 8)], sems.at[7])
    for copy in copies + [blocks_low, blocks_high]:
        copy.start()
    fine_rhs[...] = line_operand(fine_ref)
    coarse_rhs[...] = line_operand(coarse_ref)

    def spread(block, row):
        plain_m[CELL_BLOCK * block : CELL_BLOCK * (block + 1), :] = jnp.broadcast_to(row, (CELL_BLOCK, NY))

    count = blocks_ref.shape[0]
    for b in range(count):
        spread(HALO_BLOCKS + b, blocks_ref[b : b + 1, :])
    blocks_low.wait()
    blocks_high.wait()
    for b in range(HALO_BLOCKS):
        spread(b, still_ref[8 - HALO_BLOCKS + b : 9 - HALO_BLOCKS + b, :])
        spread(HALO_BLOCKS + count + b, still_ref[8 + b : 9 + b, :])
    for copy in copies:
        copy.wait()
    corner = pl.multiple_of(group * (slab // windows_ref.shape[0]) + (HALO - (WINDOW - slab // windows_ref.shape[0]) // 2), 16)
    taken = [
        pltpu.make_async_copy(plain_m.at[pl.ds(corner, WINDOW)], base_window_ref, sems.at[0]),
        pltpu.make_async_copy(plain_q.at[pl.ds(corner, WINDOW)], source_window_ref, sems.at[1]),
    ]
    for copy in taken:
        copy.start()
    for plain, ref in ((plain_u, u_ref), (plain_q, source_ref), (plain_m, base_ref)):
        for t in range(tiles):
            ref[8 * t : 8 * t + 8, :] = plain[pl.ds(t, 8, stride=tiles), :]

    first, second = divmod(HALO - 1, tiles), divmod(HALO + slab, tiles)
    walls = [(first[1], wall(space == 0, first[0])), (second[1], wall(space == ends, second[0]))]
    chunk = 28
    fields = (u_ref, base_ref, source_ref, still_ref, slope_ref, w_ref)

    def store_own(begin, size, value):
        own_ref[begin : begin + size, :] = value

    def store_u(begin, size, value):
        u_ref[begin : begin + size, :] = value

    advance(tiles, chunk, *fields, coarse_rhs, COARSE_C, COARSE_R, COARSE_Q, walls, store_own)

    def step(_, carry):
        advance(tiles, chunk, *fields, fine_rhs, FINE_C, FINE_R, 1.0, walls, store_u)
        return carry

    lax.fori_loop(0, STEPS, step, 0)
    for t in range(tiles):
        rows = slice(8 * t, 8 * t + 8)
        value = u_ref[rows, :]
        value = jnp.where(group == 0, value, value - own_ref[rows, :])
        own_ref[rows, :] = value
        plain_u[pl.ds(t, 8, stride=tiles), :] = value
    parts = windows_ref.shape[0]
    each = slab // parts
    out = [
        pltpu.make_async_copy(
            plain_u.at[pl.ds(each * k + HALO - (WINDOW - each) // 2, WINDOW)], windows_ref.at[k], window_sems.at[k]
        )
        for k in range(parts)
    ]
    for copy in out:
        copy.start()
    for copy in taken + out:
        copy.wait()


def fine_phase(parts, ends, low, high, start, heat, blocks, fine_line, coarse_line):
    total = start.shape[0] + 2 * HALO
    field = jax.ShapeDtypeStruct((total, NY), jnp.float32)
    window = jax.ShapeDtypeStruct((WINDOW, NY), jnp.float32)
    return pl.pallas_call(
        functools.partial(fine_kernel, ends),
        out_shape=(jax.ShapeDtypeStruct((parts, WINDOW, NY), jnp.float32), field, field, field, window, window),
        in_specs=[ANYWHERE] * 4 + [whole(blocks.shape), whole((NY, NY)), whole((NY, NY))],
        out_specs=(ANYWHERE, whole(field.shape), whole(field.shape), whole(field.shape), ANYWHERE, ANYWHERE),
        scratch_shapes=[pltpu.VMEM((total, NY), jnp.float32)] * 7
        + [pltpu.VMEM((2 * NY, 2 * NY), jnp.bfloat16)] * 2
        + [pltpu.SemaphoreType.DMA((8,)), pltpu.SemaphoreType.DMA((parts,))],
        compiler_params=pltpu.CompilerParams(vmem_limit_bytes=VMEM_LIMIT),
        name="fine_phase",
    )(low, high, start, heat, blocks, fine_line, coarse_line)


def sweep_kernel(ends, jumps_ref, base_window_ref, source_window_ref, coarse_ref, back_ref, u_ref, base_ref, source_ref, still_ref, slope_ref, w_ref, plain, rhs):
    parts = jumps_ref.shape[0]
    space, part = lax.axis_index("space"), lax.axis_index("tm")
    tiles = WINDOW // 8
    rhs[...] = line_operand(coarse_ref)
    for t in range(tiles):
        rows = slice(8 * t, 8 * t + 8)
        base_ref[rows, :] = base_window_ref[pl.ds(t, 8, stride=tiles), :]
        source_ref[rows, :] = source_window_ref[pl.ds(t, 8, stride=tiles), :]
        u_ref[rows, :] = jumps_ref[0, pl.ds(t, 8, stride=tiles), :]
    back_ref[0] = jnp.zeros((BACK, NY), jnp.float32)
    back_ref[1] = jumps_ref[0, MARGIN : MARGIN + BACK, :]
    each = WINDOW // 2
    reach = (WINDOW - each) // 2
    first, second = divmod(reach - 1, tiles), divmod(reach + each, tiles)
    walls = [
        (first[1], wall((space == 0) & (part == 0), first[0])),
        (second[1], wall((space == ends) & (part == parts - 1), second[0])),
    ]
    fields = (u_ref, base_ref, source_ref, still_ref, slope_ref, w_ref)

    def turn(g, carry):
        def store(begin, size, value):
            for n in range(size // 8):
                t = begin // 8 + n
                moved = value[8 * n : 8 * n + 8] + jumps_ref[g, pl.ds(t, 8, stride=tiles), :]
                u_ref[8 * t : 8 * t + 8, :] = moved
                plain[pl.ds(t, 8, stride=tiles), :] = moved

        advance(tiles, tiles, *fields, rhs, COARSE_C, COARSE_R, COARSE_Q, walls, store)
        back_ref[g + 1] = plain[MARGIN : MARGIN + BACK, :]
        return carry

    lax.fori_loop(1, parts - 1, turn, 0)


def sweep(ends, jumps, base_window, source_window, coarse_line):
    parts = jumps.shape[0]
    window = pltpu.VMEM((WINDOW, NY), jnp.float32)
    return pl.pallas_call(
        functools.partial(sweep_kernel, ends),
        out_shape=jax.ShapeDtypeStruct((parts, BACK, NY), jnp.float32),
        in_specs=[whole(jumps.shape), whole((WINDOW, NY)), whole((WINDOW, NY)), whole((NY, NY))],
        out_specs=whole((parts, BACK, NY)),
        scratch_shapes=[window] * 7 + [pltpu.VMEM((2 * NY, 2 * NY), jnp.bfloat16)],
        compiler_params=pltpu.CompilerParams(vmem_limit_bytes=VMEM_LIMIT),
        name="sweep",
    )(jumps, base_window, source_window, coarse_line)


def last_kernel(
    ends, parts_ref, own_ref, base_ref, source_ref, start_ref, coarse_ref, ends_ref, next_ref, plain, u_ref, still_ref, slope_ref, w_ref, rhs
):
    space, group = lax.axis_index("space"), lax.axis_index("tm")
    parts = parts_ref.shape[0]
    slab = next_ref.shape[0]
    total = slab + 2 * HALO
    tiles = total // 8
    each = slab // parts
    side = (BACK - each) // 2
    rhs[...] = line_operand(coarse_ref)
    empty = jnp.zeros((HALO - 8, NY), jnp.float32)
    plain[0 : HALO - 8, :] = empty
    plain[total - HALO + 8 :, :] = empty
    gap = jnp.zeros((8 - side, NY), jnp.float32)
    plain[HALO - 8 : HALO, :] = jnp.concatenate([gap, parts_ref[0, 0:side, :]], axis=0)
    plain[HALO + slab : HALO + slab + 8, :] = jnp.concatenate([parts_ref[parts - 1, BACK - side : BACK, :], gap], axis=0)
    for k in range(parts):
        value = parts_ref[k, side : side + each, :]
        plain[HALO + each * k : HALO + each * (k + 1), :] = value
        rows = slice(each * k, each * (k + 1))
        next_ref[rows, :] = jnp.where(group == 0, start_ref[rows, :], value)
    for t in range(tiles):
        u_ref[8 * t : 8 * t + 8, :] = plain[pl.ds(t, 8, stride=tiles), :]
    first, second = divmod(HALO - 1, tiles), divmod(HALO + slab, tiles)
    walls = [(first[1], wall(space == 0, first[0])), (second[1], wall(space == ends, second[0]))]

    def store(begin, size, value):
        for n in range(size // 8):
            t = begin // 8 + n
            own = own_ref[8 * t : 8 * t + 8, :]
            moved = value[8 * n : 8 * n + 8]
            plain[pl.ds(t, 8, stride=tiles), :] = jnp.where(group == 0, own, moved + own)

    fields = (u_ref, base_ref, source_ref, still_ref, slope_ref, w_ref)
    advance(tiles, 28, *fields, rhs, COARSE_C, COARSE_R, COARSE_Q, walls, store)
    ends_ref[...] = plain[HALO : HALO + slab, :]


def last_step(ends, back, own, base, source, start, coarse_line):
    field = jax.ShapeDtypeStruct(start.shape, jnp.float32)
    total = own.shape
    return pl.pallas_call(
        functools.partial(last_kernel, ends),
        out_shape=(field, field),
        in_specs=[whole(back.shape), whole(total), whole(total), whole(total), whole(start.shape), whole((NY, NY))],
        out_specs=(whole(start.shape), whole(start.shape)),
        scratch_shapes=[pltpu.VMEM(total, jnp.float32)] * 5 + [pltpu.VMEM((2 * NY, 2 * NY), jnp.bfloat16)],
        compiler_params=pltpu.CompilerParams(vmem_limit_bytes=VMEM_LIMIT),
        name="last_step",
    )(back, own, base, source, start, coarse_line)


def on_device(starts, region, viscosity, heat_source, fine_line, coarse_line):
    start = starts[0]
    parts = lax.axis_size("tm")
    ends = lax.axis_size("space") - 1
    head, tail, blocks = pack(viscosity, region, start, heat_source)
    low = lax.ppermute(tail, "space", [(i, i + 1) for i in range(ends)])
    high = lax.ppermute(head, "space", [(i + 1, i) for i in range(ends)])
    windows, own, base, source, base_window, source_window = fine_phase(
        parts, ends, low, high, start, heat_source, blocks, fine_line, coarse_line
    )
    jumps = lax.all_to_all(windows, "tm", 0, 0)
    back = sweep(ends, jumps, base_window, source_window, coarse_line)
    mine = lax.all_to_all(back, "tm", 0, 0)
    value, following = last_step(ends, mine, own, base, source, start, coarse_line)
    return value[None], following[None]


def solution(mesh):
    placed = (P("tm", "space", None), P("space", None), P(), P("space", None), P(), P())
    return jax.shard_map(
        on_device,
        mesh=mesh,
        in_specs=placed,
        out_specs=(P("tm", "space", None), P("tm", "space", None)),
        check_vma=False,
    )
```

```python
import functools

import jax
import jax.numpy as jnp
from jax import lax
from jax.experimental import pallas as pl
from jax.experimental.pallas import tpu as pltpu
from jax.sharding import PartitionSpec as P

NY = 128
CELL_BLOCK = 16
REGIONS = 8
STEPS = 8

FINE_C = 0.3
FINE_R = 0.2
COARSE_C = 0.5
COARSE_R = 0.12
COARSE_Q = 3.0

HALO = 48
HALO_BLOCKS = HALO // CELL_BLOCK
PACK = 2 * HALO + 8
WINDOW = 128
MARGIN = 28
BACK = WINDOW - 2 * MARGIN
GROUPS_OF_TILES = 6
VMEM_LIMIT = 16 * 1024 * 1024
SMALL_VMEM_LIMIT = 4 * 1024 * 1024


def from_left(tile):
    return pltpu.roll(tile, 1, 0)


def from_right(tile):
    return pltpu.roll(tile, 7, 0)


def halves(x):
    high = x.astype(jnp.bfloat16)
    low = (x - high.astype(jnp.float32)).astype(jnp.bfloat16)
    return high, low


def line_operand(line_ref):
    high, low = halves(line_ref[...].T)
    top = jnp.concatenate([high, low], axis=1)
    return jnp.concatenate([top, top], axis=0)


def product(pairs, rhs_ref):
    left = jnp.concatenate([jnp.concatenate(halves(e), axis=1) for e in pairs], axis=0)
    both = jnp.dot(left, rhs_ref[...], preferred_element_type=jnp.float32)
    return both[:, :NY] + both[:, NY:]


def rotated(pairs, count, turn):
    cuts = [pairs * n // count for n in range(count + 1)]
    groups = [list(range(cuts[n], cuts[n + 1])) for n in range(count)]
    return groups[turn:] + groups[:turn]


def flux_pass(groups, viscosity_of, slope_of, base_of, walls, rhs_ref, store):
    order = [i for group in groups for i in group]
    pairs = len(order)
    begin, prior = order[0], order[-1]
    m_begin = m = viscosity_of(begin)
    top = m[:8]
    if begin == 0:
        top = from_right(top)
    before = (viscosity_of(prior)[8:] + top) * slope_of(prior)[8:]
    if begin == 0:
        before = from_left(before)
    n = 0
    for group in groups:
        done = []
        for i in group:
            n += 1
            following = m_begin if n == pairs else viscosity_of(order[n])
            top = following[:8]
            if i + 1 == pairs:
                top = from_right(top)
            flux = (m + jnp.concatenate([m[8:], top], axis=0)) * slope_of(i)
            e = base_of(i) + (flux - jnp.concatenate([before, flux[:8]], axis=0))
            for tile, mask in walls:
                if tile // 2 == i:
                    ones = jnp.ones_like(mask)
                    both = [mask, ones] if tile % 2 == 0 else [ones, mask]
                    e = e * jnp.concatenate(both, axis=0)
            before = flux[8:]
            if i + 1 == pairs:
                before = from_left(before)
            m = following
            done.append(e)
        store(16 * group[0], 16 * len(group), product(done, rhs_ref))


def advance(tiles, parts, u_ref, base_ref, heat_ref, still_ref, slope_ref, w_ref, rhs_ref, courant, ratio, weight, walls, store):
    pairs = tiles // 2

    def rows(i):
        return slice(16 * i, 16 * i + 16)

    def viscosity_first(i):
        u = u_ref[rows(i), :]
        return base_ref[rows(i), :] / (2.0 + u * u)

    def viscosity_second(i):
        u = 0.5 * (u_ref[rows(i), :] + w_ref[rows(i), :])
        return base_ref[rows(i), :] / (2.0 + u * u)

    right = from_right(u_ref[0:8, :])

    def step_up(i):
        u = u_ref[rows(i), :]
        if i + 1 < pairs:
            above = u_ref[16 * i + 8 : 16 * i + 24, :]
        else:
            above = jnp.concatenate([u[8:], right], axis=0)
        return above - u

    def slope_first(i):
        return ratio * step_up(i)

    def still_first(i):
        up = step_up(i)
        slope_ref[rows(i), :] = ratio * up
        prior = from_left(step_up(pairs - 1)[8:]) if i == 0 else step_up(i - 1)[8:]
        heat = heat_ref[rows(i), :]
        if weight != 1.0:
            heat = weight * heat
        still = (u_ref[rows(i), :] + heat) - courant * jnp.concatenate([prior, up[:8]], axis=0)
        still_ref[rows(i), :] = still
        return still

    def store_first(start, count, value):
        w_ref[start : start + count, :] = value

    flux_pass(rotated(pairs, parts, 0), viscosity_first, slope_first, still_first, walls, rhs_ref, store_first)
    flux_pass(
        rotated(pairs, parts, parts // 2),
        viscosity_second,
        lambda i: slope_ref[rows(i), :],
        lambda i: still_ref[rows(i), :],
        walls,
        rhs_ref,
        store,
    )


def wall(at_wall, sublane):
    row = lax.broadcasted_iota(jnp.int32, (8, NY), 0)
    return jnp.where((row == sublane) & at_wall, 0.0, 1.0)


def whole(shape):
    return pl.BlockSpec(shape, lambda: (0,) * len(shape))


ANYWHERE = pl.BlockSpec(memory_space=pl.ANY)


def spread_blocks(viscosity_ref, region_ref):
    region = region_ref[...]
    count = region.shape[1]
    picked = jnp.zeros(region.shape, jnp.float32)
    for value in range(REGIONS):
        picked = jnp.where(region == value, viscosity_ref[value], picked)
    wide = jnp.concatenate([picked, jnp.zeros((region.shape[0], NY - count), jnp.float32)], axis=1)
    cells = [jnp.broadcast_to(wide[n : n + 1], (CELL_BLOCK, NY)) for n in range(NY // CELL_BLOCK)]
    return jnp.concatenate(cells, axis=0).T[:count]


def stay(*arrays):
    return [pltpu.with_memory_space_constraint(x, pltpu.HBM) for x in arrays]


def pack_kernel(viscosity_ref, region_ref, start_ref, heat_ref, head_ref, tail_ref, sems):
    slab = start_ref.shape[0]
    copies = []
    for n, (edge, first) in enumerate(((tail_ref, slab - HALO), (head_ref, 0))):
        for m, field in enumerate((start_ref, heat_ref)):
            target = edge.at[pl.ds(m * HALO, HALO)]
            copies.append(pltpu.make_async_copy(field.at[pl.ds(first, HALO)], target, sems.at[2 * n + m]))
    for copy in copies:
        copy.start()
    spread = spread_blocks(viscosity_ref, region_ref)
    head_ref[2 * HALO :, :] = spread[:8]
    tail_ref[2 * HALO :, :] = spread[spread.shape[0] - 8 :]
    for copy in copies:
        copy.wait()


def pack(viscosity, region, start, heat):
    edge = (PACK, NY)
    return pl.pallas_call(
        pack_kernel,
        out_shape=(jax.ShapeDtypeStruct(edge, jnp.float32), jax.ShapeDtypeStruct(edge, jnp.float32)),
        in_specs=[pl.BlockSpec(memory_space=pltpu.SMEM), whole(region.shape), ANYWHERE, ANYWHERE],
        out_specs=(whole(edge), whole(edge)),
        scratch_shapes=[pltpu.SemaphoreType.DMA((4,))],
        compiler_params=pltpu.CompilerParams(vmem_limit_bytes=SMALL_VMEM_LIMIT),
        name="pack",
    )(viscosity, region, start, heat)


def stage_kernel(viscosity_ref, region_ref, fine_ref, coarse_ref, fine_rhs, coarse_rhs, base_ref):
    spread = spread_blocks(viscosity_ref, region_ref)
    for b in range(spread.shape[0]):
        base_ref[CELL_BLOCK * b : CELL_BLOCK * (b + 1), :] = jnp.broadcast_to(spread[b : b + 1], (CELL_BLOCK, NY))
    fine_rhs[...] = line_operand(fine_ref)
    coarse_rhs[...] = line_operand(coarse_ref)


def stage(viscosity, region, fine_line, coarse_line):
    rows = region.shape[1] * CELL_BLOCK
    square = (2 * NY, 2 * NY)
    return pl.pallas_call(
        stage_kernel,
        out_shape=(
            jax.ShapeDtypeStruct(square, jnp.bfloat16),
            jax.ShapeDtypeStruct(square, jnp.bfloat16),
            jax.ShapeDtypeStruct((rows, NY), jnp.float32),
        ),
        in_specs=[pl.BlockSpec(memory_space=pltpu.SMEM), whole(region.shape), whole((NY, NY)), whole((NY, NY))],
        out_specs=(whole(square), whole(square), whole((rows, NY))),
        compiler_params=pltpu.CompilerParams(vmem_limit_bytes=SMALL_VMEM_LIMIT),
        cost_estimate=pl.CostEstimate(flops=rows * NY, bytes_accessed=8 * rows * NY, transcendentals=0),
        name="stage",
    )(viscosity, region, fine_line, coarse_line)


def fine_kernel(
    ends,
    low_ref,
    high_ref,
    start_ref,
    heat_ref,
    middle_ref,
    fine_rhs,
    coarse_rhs,
    windows_ref,
    own_ref,
    base_ref,
    source_ref,
    base_window_ref,
    source_window_ref,
    plain_u,
    plain_q,
    plain_m,
    u_ref,
    still_ref,
    slope_ref,
    w_ref,
):
    space, group = lax.axis_index("space"), lax.axis_index("tm")
    slab = start_ref.shape[0]
    total = slab + 2 * HALO
    tiles = total // 8
    for plain, part, middle in ((plain_u, 0, start_ref), (plain_q, HALO, heat_ref)):
        plain[0:HALO, :] = low_ref[part : part + HALO, :]
        plain[HALO : HALO + slab, :] = middle[...]
        plain[HALO + slab :, :] = high_ref[part : part + HALO, :]
    plain_m[HALO : HALO + slab, :] = middle_ref[...]
    for b in range(HALO_BLOCKS):
        left, right = 2 * HALO + 8 - HALO_BLOCKS + b, 2 * HALO + b
        rows = slice(CELL_BLOCK * b, CELL_BLOCK * (b + 1))
        plain_m[rows, :] = jnp.broadcast_to(low_ref[left : left + 1, :], (CELL_BLOCK, NY))
        rows = slice(HALO + slab + CELL_BLOCK * b, HALO + slab + CELL_BLOCK * (b + 1))
        plain_m[rows, :] = jnp.broadcast_to(high_ref[right : right + 1, :], (CELL_BLOCK, NY))
    parts = windows_ref.shape[0]
    each = slab // parts
    reach = (WINDOW - each) // 2
    corner = pl.multiple_of(group * each + (HALO - reach), CELL_BLOCK)
    base_window_ref[...] = plain_m[pl.ds(corner, WINDOW), :]
    source_window_ref[...] = plain_q[pl.ds(corner, WINDOW), :]
    for plain, ref in ((plain_u, u_ref), (plain_q, source_ref), (plain_m, base_ref)):
        for t in range(tiles):
            ref[8 * t : 8 * t + 8, :] = plain[pl.ds(t, 8, stride=tiles), :]

    first, second = divmod(HALO - 1, tiles), divmod(HALO + slab, tiles)
    walls = [(first[1], wall(space == 0, first[0])), (second[1], wall(space == ends, second[0]))]
    fields = (u_ref, base_ref, source_ref, still_ref, slope_ref, w_ref)

    def store_own(begin, size, value):
        own_ref[begin : begin + size, :] = value

    def store_u(begin, size, value):
        u_ref[begin : begin + size, :] = value

    advance(tiles, GROUPS_OF_TILES, *fields, coarse_rhs, COARSE_C, COARSE_R, COARSE_Q, walls, store_own)

    def step(_, carry):
        advance(tiles, GROUPS_OF_TILES, *fields, fine_rhs, FINE_C, FINE_R, 1.0, walls, store_u)
        return carry

    lax.fori_loop(0, STEPS, step, 0, unroll=4)
    for t in range(tiles):
        rows = slice(8 * t, 8 * t + 8)
        value = u_ref[rows, :]
        value = jnp.where(group == 0, value, value - own_ref[rows, :])
        own_ref[rows, :] = value
        plain_u[pl.ds(t, 8, stride=tiles), :] = value
    for k in range(parts):
        first = each * k + HALO - reach
        windows_ref[k] = plain_u[first : first + WINDOW, :]


def fine_phase(parts, ends, low, high, start, heat, base, fine_rhs, coarse_rhs):
    total = start.shape[0] + 2 * HALO
    operands = (low, high, start, heat, base, fine_rhs, coarse_rhs)
    field = jax.ShapeDtypeStruct((total, NY), jnp.float32)
    window = jax.ShapeDtypeStruct((WINDOW, NY), jnp.float32)
    return pl.pallas_call(
        functools.partial(fine_kernel, ends),
        out_shape=(jax.ShapeDtypeStruct((parts, WINDOW, NY), jnp.float32), field, field, field, window, window),
        in_specs=[whole(x.shape) for x in operands],
        out_specs=(whole((parts, WINDOW, NY)), *[whole(field.shape)] * 3, *[whole(window.shape)] * 2),
        scratch_shapes=[pltpu.VMEM((total, NY), jnp.float32)] * 7,
        compiler_params=pltpu.CompilerParams(vmem_limit_bytes=VMEM_LIMIT),
        name="fine_phase",
    )(*operands)


def sweep_kernel(ends, jumps_ref, base_window_ref, source_window_ref, rhs, back_ref, u_ref, base_ref, source_ref, still_ref, slope_ref, w_ref, plain):
    parts = jumps_ref.shape[0]
    space, part = lax.axis_index("space"), lax.axis_index("tm")
    tiles = WINDOW // 8
    for t in range(tiles):
        rows = slice(8 * t, 8 * t + 8)
        base_ref[rows, :] = base_window_ref[pl.ds(t, 8, stride=tiles), :]
        source_ref[rows, :] = source_window_ref[pl.ds(t, 8, stride=tiles), :]
        u_ref[rows, :] = jumps_ref[0, pl.ds(t, 8, stride=tiles), :]
    back_ref[0] = jnp.zeros((BACK, NY), jnp.float32)
    back_ref[1] = jumps_ref[0, MARGIN : MARGIN + BACK, :]
    each = WINDOW // 2
    reach = (WINDOW - each) // 2
    first, second = divmod(reach - 1, tiles), divmod(reach + each, tiles)
    walls = [
        (first[1], wall((space == 0) & (part == 0), first[0])),
        (second[1], wall((space == ends) & (part == parts - 1), second[0])),
    ]
    fields = (u_ref, base_ref, source_ref, still_ref, slope_ref, w_ref)

    def turn(g, carry):
        def store(begin, size, value):
            for n in range(size // 8):
                t = begin // 8 + n
                moved = value[8 * n : 8 * n + 8] + jumps_ref[g, pl.ds(t, 8, stride=tiles), :]
                u_ref[8 * t : 8 * t + 8, :] = moved
                plain[pl.ds(t, 8, stride=tiles), :] = moved

        advance(tiles, 1, *fields, rhs, COARSE_C, COARSE_R, COARSE_Q, walls, store)
        back_ref[g + 1] = plain[MARGIN : MARGIN + BACK, :]
        return carry

    lax.fori_loop(1, parts - 1, turn, 0)


def sweep(ends, jumps, base_window, source_window, coarse_rhs):
    parts = jumps.shape[0]
    window = pltpu.VMEM((WINDOW, NY), jnp.float32)
    return pl.pallas_call(
        functools.partial(sweep_kernel, ends),
        out_shape=jax.ShapeDtypeStruct((parts, BACK, NY), jnp.float32),
        in_specs=[whole(jumps.shape), whole((WINDOW, NY)), whole((WINDOW, NY)), whole(coarse_rhs.shape)],
        out_specs=whole((parts, BACK, NY)),
        scratch_shapes=[window] * 7,
        compiler_params=pltpu.CompilerParams(vmem_limit_bytes=VMEM_LIMIT),
        name="sweep",
    )(jumps, base_window, source_window, coarse_rhs)


def last_kernel(
    ends, parts_ref, own_ref, base_ref, source_ref, start_ref, rhs, ends_ref, next_ref, plain, u_ref, still_ref, slope_ref, w_ref
):
    space, group = lax.axis_index("space"), lax.axis_index("tm")
    parts = parts_ref.shape[0]
    slab = next_ref.shape[0]
    total = slab + 2 * HALO
    tiles = total // 8
    each = slab // parts
    side = (BACK - each) // 2
    empty = jnp.zeros((HALO - 8, NY), jnp.float32)
    plain[0 : HALO - 8, :] = empty
    plain[total - HALO + 8 :, :] = empty
    gap = jnp.zeros((8 - side, NY), jnp.float32)
    plain[HALO - 8 : HALO, :] = jnp.concatenate([gap, parts_ref[0, 0:side, :]], axis=0)
    plain[HALO + slab : HALO + slab + 8, :] = jnp.concatenate([parts_ref[parts - 1, BACK - side : BACK, :], gap], axis=0)
    for k in range(parts):
        value = parts_ref[k, side : side + each, :]
        plain[HALO + each * k : HALO + each * (k + 1), :] = value
        rows = slice(each * k, each * (k + 1))
        next_ref[rows, :] = jnp.where(group == 0, start_ref[rows, :], value)
    for t in range(tiles):
        u_ref[8 * t : 8 * t + 8, :] = plain[pl.ds(t, 8, stride=tiles), :]
    first, second = divmod(HALO - 1, tiles), divmod(HALO + slab, tiles)
    walls = [(first[1], wall(space == 0, first[0])), (second[1], wall(space == ends, second[0]))]

    def store(begin, size, value):
        for n in range(size // 8):
            t = begin // 8 + n
            own = own_ref[8 * t : 8 * t + 8, :]
            moved = value[8 * n : 8 * n + 8]
            plain[pl.ds(t, 8, stride=tiles), :] = jnp.where(group == 0, own, moved + own)

    fields = (u_ref, base_ref, source_ref, still_ref, slope_ref, w_ref)
    advance(tiles, GROUPS_OF_TILES, *fields, rhs, COARSE_C, COARSE_R, COARSE_Q, walls, store)
    ends_ref[...] = plain[HALO : HALO + slab, :]


def last_step(ends, back, own, base, source, start, coarse_rhs):
    field = jax.ShapeDtypeStruct(start.shape, jnp.float32)
    total = own.shape
    return pl.pallas_call(
        functools.partial(last_kernel, ends),
        out_shape=(field, field),
        in_specs=[whole(back.shape), whole(total), whole(total), whole(total), whole(start.shape), whole(coarse_rhs.shape)],
        out_specs=(whole(start.shape), whole(start.shape)),
        scratch_shapes=[pltpu.VMEM(total, jnp.float32)] * 5,
        compiler_params=pltpu.CompilerParams(vmem_limit_bytes=VMEM_LIMIT),
        name="last_step",
    )(back, own, base, source, start, coarse_rhs)


def on_device(starts, region, viscosity, heat_source, fine_line, coarse_line):
    start = starts[0]
    parts = lax.axis_size("tm")
    ends = lax.axis_size("space") - 1
    head, tail = pack(*stay(viscosity, region.T, start, heat_source))
    low = lax.ppermute(tail, "space", [(i, i + 1) for i in range(ends)])
    high = lax.ppermute(head, "space", [(i + 1, i) for i in range(ends)])
    fine_rhs, coarse_rhs, middle = stage(*stay(viscosity, region.T, fine_line, coarse_line))
    windows, own, base, source, base_window, source_window = fine_phase(
        parts, ends, low, high, start, heat_source, middle, fine_rhs, coarse_rhs
    )
    jumps = lax.all_to_all(windows, "tm", 0, 0)
    back = sweep(ends, jumps, base_window, source_window, coarse_rhs)
    mine = lax.all_to_all(back, "tm", 0, 0)
    value, following = last_step(ends, mine, own, base, source, start, coarse_rhs)
    return value[None], following[None]


def solution(mesh):
    placed = (P("tm", "space", None), P("space", None), P(), P("space", None), P(), P())
    return jax.shard_map(
        on_device,
        mesh=mesh,
        in_specs=placed,
        out_specs=(P("tm", "space", None), P("tm", "space", None)),
        check_vma=False,
    )
```

```python
import functools

import jax
import jax.numpy as jnp
from jax import lax
from jax.experimental import pallas as pl
from jax.experimental.pallas import tpu as pltpu
from jax.sharding import PartitionSpec as P

NY = 128
CELL_BLOCK = 16
REGIONS = 8
STEPS = 8

FINE_C = 0.3
FINE_R = 0.2
COARSE_C = 0.5
COARSE_R = 0.12
COARSE_Q = 3.0

HALO = 48
HALO_BLOCKS = HALO // CELL_BLOCK
PACK = 2 * HALO + 8
WINDOW = 192
MARGIN = 28
BACK = WINDOW - 2 * MARGIN
BLOCKS = 2
GROUPS_OF_TILES = 6
SWEEP_GROUPS_OF_TILES = 2
VMEM_LIMIT = 16 * 1024 * 1024
SMALL_VMEM_LIMIT = 4 * 1024 * 1024


def from_left(tile):
    return pltpu.roll(tile, 1, 0)


def from_right(tile):
    return pltpu.roll(tile, 7, 0)


def halves(x):
    high = x.astype(jnp.bfloat16)
    low = (x - high.astype(jnp.float32)).astype(jnp.bfloat16)
    return high, low


def line_operand(line_ref):
    high, low = halves(line_ref[...].T)
    top = jnp.concatenate([high, low], axis=1)
    return jnp.concatenate([top, top], axis=0)


def product(pairs, rhs_ref):
    left = jnp.concatenate([jnp.concatenate(halves(e), axis=1) for e in pairs], axis=0)
    both = jnp.dot(left, rhs_ref[...], preferred_element_type=jnp.float32)
    return both[:, :NY] + both[:, NY:]


def rotated(pairs, count, turn):
    cuts = [pairs * n // count for n in range(count + 1)]
    groups = [list(range(cuts[n], cuts[n + 1])) for n in range(count)]
    return groups[turn:] + groups[:turn]


def flux_pass(groups, viscosity_of, slope_of, base_of, walls, rhs_ref, store):
    order = [i for group in groups for i in group]
    pairs = len(order)
    begin, prior = order[0], order[-1]
    m_begin = m = viscosity_of(begin)
    top = m[:8]
    if begin == 0:
        top = from_right(top)
    before = (viscosity_of(prior)[8:] + top) * slope_of(prior)[8:]
    if begin == 0:
        before = from_left(before)
    n = 0
    for group in groups:
        done = []
        for i in group:
            n += 1
            following = m_begin if n == pairs else viscosity_of(order[n])
            top = following[:8]
            if i + 1 == pairs:
                top = from_right(top)
            flux = (m + jnp.concatenate([m[8:], top], axis=0)) * slope_of(i)
            e = base_of(i) + (flux - jnp.concatenate([before, flux[:8]], axis=0))
            for tile, mask in walls:
                if tile // 2 == i:
                    ones = jnp.ones_like(mask)
                    both = [mask, ones] if tile % 2 == 0 else [ones, mask]
                    e = e * jnp.concatenate(both, axis=0)
            before = flux[8:]
            if i + 1 == pairs:
                before = from_left(before)
            m = following
            done.append(e)
        store(16 * group[0], 16 * len(group), product(done, rhs_ref))


def advance(tiles, parts, u_ref, base_ref, heat_ref, still_ref, slope_ref, w_ref, rhs_ref, courant, ratio, weight, walls, store):
    pairs = tiles // 2

    def rows(i):
        return slice(16 * i, 16 * i + 16)

    def viscosity_first(i):
        u = u_ref[rows(i), :]
        return base_ref[rows(i), :] / (2.0 + u * u)

    def viscosity_second(i):
        u = 0.5 * (u_ref[rows(i), :] + w_ref[rows(i), :])
        return base_ref[rows(i), :] / (2.0 + u * u)

    right = from_right(u_ref[0:8, :])

    def step_up(i):
        u = u_ref[rows(i), :]
        if i + 1 < pairs:
            above = u_ref[16 * i + 8 : 16 * i + 24, :]
        else:
            above = jnp.concatenate([u[8:], right], axis=0)
        return above - u

    def slope_first(i):
        return ratio * step_up(i)

    def still_first(i):
        up = step_up(i)
        slope_ref[rows(i), :] = ratio * up
        prior = from_left(step_up(pairs - 1)[8:]) if i == 0 else step_up(i - 1)[8:]
        heat = heat_ref[rows(i), :]
        if weight != 1.0:
            heat = weight * heat
        still = (u_ref[rows(i), :] + heat) - courant * jnp.concatenate([prior, up[:8]], axis=0)
        still_ref[rows(i), :] = still
        return still

    def store_first(start, count, value):
        w_ref[start : start + count, :] = value

    flux_pass(rotated(pairs, parts, 0), viscosity_first, slope_first, still_first, walls, rhs_ref, store_first)
    flux_pass(
        rotated(pairs, parts, parts // 2),
        viscosity_second,
        lambda i: slope_ref[rows(i), :],
        lambda i: still_ref[rows(i), :],
        walls,
        rhs_ref,
        store,
    )


def wall(at_wall, sublane):
    row = lax.broadcasted_iota(jnp.int32, (8, NY), 0)
    return jnp.where((row == sublane) & at_wall, 0.0, 1.0)


def mirrored(part, parts):
    return (parts // 2 - 1 - part // 2) * 2 + part % 2


def placed(second, part, parts):
    return jnp.where(second, mirrored(part, parts), part)


def whole(shape):
    return pl.BlockSpec(shape, lambda: (0,) * len(shape))


ANYWHERE = pl.BlockSpec(memory_space=pl.ANY)


def spread_blocks(viscosity_ref, region_ref):
    region = region_ref[...]
    count = region.shape[1]
    picked = jnp.zeros(region.shape, jnp.float32)
    for value in range(REGIONS):
        picked = jnp.where(region == value, viscosity_ref[value], picked)
    wide = jnp.concatenate([picked, jnp.zeros((region.shape[0], NY - count), jnp.float32)], axis=1)
    cells = [jnp.broadcast_to(wide[n : n + 1], (CELL_BLOCK, NY)) for n in range(NY // CELL_BLOCK)]
    return jnp.concatenate(cells, axis=0).T[:count]


def stay(*arrays):
    return [pltpu.with_memory_space_constraint(x, pltpu.HBM) for x in arrays]


def pack_kernel(viscosity_ref, region_ref, start_ref, heat_ref, head_ref, tail_ref, sems):
    slab = start_ref.shape[0]
    copies = []
    for n, (edge, first) in enumerate(((tail_ref, slab - HALO), (head_ref, 0))):
        for m, field in enumerate((start_ref, heat_ref)):
            target = edge.at[pl.ds(m * HALO, HALO)]
            copies.append(pltpu.make_async_copy(field.at[pl.ds(first, HALO)], target, sems.at[2 * n + m]))
    for copy in copies:
        copy.start()
    spread = spread_blocks(viscosity_ref, region_ref)
    head_ref[2 * HALO :, :] = spread[:8]
    tail_ref[2 * HALO :, :] = spread[spread.shape[0] - 8 :]
    for copy in copies:
        copy.wait()


def pack(viscosity, region, start, heat):
    edge = (PACK, NY)
    return pl.pallas_call(
        pack_kernel,
        out_shape=(jax.ShapeDtypeStruct(edge, jnp.float32), jax.ShapeDtypeStruct(edge, jnp.float32)),
        in_specs=[pl.BlockSpec(memory_space=pltpu.SMEM), whole(region.shape), ANYWHERE, ANYWHERE],
        out_specs=(whole(edge), whole(edge)),
        scratch_shapes=[pltpu.SemaphoreType.DMA((4,))],
        compiler_params=pltpu.CompilerParams(vmem_limit_bytes=SMALL_VMEM_LIMIT),
        name="pack",
    )(viscosity, region, start, heat)


def stage_kernel(viscosity_ref, region_ref, fine_ref, coarse_ref, fine_rhs, coarse_rhs, base_ref):
    spread = spread_blocks(viscosity_ref, region_ref)
    for b in range(spread.shape[0]):
        base_ref[CELL_BLOCK * b : CELL_BLOCK * (b + 1), :] = jnp.broadcast_to(spread[b : b + 1], (CELL_BLOCK, NY))
    fine_rhs[...] = line_operand(fine_ref)
    coarse_rhs[...] = line_operand(coarse_ref)


def stage(viscosity, region, fine_line, coarse_line):
    rows = region.shape[1] * CELL_BLOCK
    square = (2 * NY, 2 * NY)
    return pl.pallas_call(
        stage_kernel,
        out_shape=(
            jax.ShapeDtypeStruct(square, jnp.bfloat16),
            jax.ShapeDtypeStruct(square, jnp.bfloat16),
            jax.ShapeDtypeStruct((rows, NY), jnp.float32),
        ),
        in_specs=[pl.BlockSpec(memory_space=pltpu.SMEM), whole(region.shape), whole((NY, NY)), whole((NY, NY))],
        out_specs=(whole(square), whole(square), whole((rows, NY))),
        compiler_params=pltpu.CompilerParams(vmem_limit_bytes=SMALL_VMEM_LIMIT),
        cost_estimate=pl.CostEstimate(flops=rows * NY, bytes_accessed=8 * rows * NY, transcendentals=0),
        name="stage",
    )(viscosity, region, fine_line, coarse_line)


def fine_kernel(
    ends,
    low_ref,
    high_ref,
    start_ref,
    heat_ref,
    middle_ref,
    fine_rhs,
    coarse_rhs,
    windows_ref,
    own_ref,
    base_ref,
    source_ref,
    base_window_ref,
    source_window_ref,
    plain_u,
    plain_q,
    plain_m,
    u_ref,
    still_ref,
    slope_ref,
    w_ref,
):
    space, group = lax.axis_index("space"), lax.axis_index("tm")
    slab = start_ref.shape[0]
    total = slab + 2 * HALO
    tiles = total // 8
    for plain, part, middle in ((plain_u, 0, start_ref), (plain_q, HALO, heat_ref)):
        plain[0:HALO, :] = low_ref[part : part + HALO, :]
        plain[HALO : HALO + slab, :] = middle[...]
        plain[HALO + slab :, :] = high_ref[part : part + HALO, :]
    plain_m[HALO : HALO + slab, :] = middle_ref[...]
    for b in range(HALO_BLOCKS):
        left, right = 2 * HALO + 8 - HALO_BLOCKS + b, 2 * HALO + b
        rows = slice(CELL_BLOCK * b, CELL_BLOCK * (b + 1))
        plain_m[rows, :] = jnp.broadcast_to(low_ref[left : left + 1, :], (CELL_BLOCK, NY))
        rows = slice(HALO + slab + CELL_BLOCK * b, HALO + slab + CELL_BLOCK * (b + 1))
        plain_m[rows, :] = jnp.broadcast_to(high_ref[right : right + 1, :], (CELL_BLOCK, NY))
    parts = windows_ref.shape[0]
    each = slab // parts
    reach = (WINDOW - each) // 2
    second = group >= parts
    place = jnp.where(second, group - parts, group)
    corner = pl.multiple_of(placed(second, place, parts) * each + (HALO - reach), CELL_BLOCK)
    base_window_ref[...] = plain_m[pl.ds(corner, WINDOW), :]
    source_window_ref[...] = plain_q[pl.ds(corner, WINDOW), :]
    for plain, ref in ((plain_u, u_ref), (plain_q, source_ref), (plain_m, base_ref)):
        for t in range(tiles):
            ref[8 * t : 8 * t + 8, :] = plain[pl.ds(t, 8, stride=tiles), :]

    under, over = divmod(HALO - 1, tiles), divmod(HALO + slab, tiles)
    walls = [(under[1], wall(space == 0, under[0])), (over[1], wall(space == ends, over[0]))]
    fields = (u_ref, base_ref, source_ref, still_ref, slope_ref, w_ref)

    def store_own(begin, size, value):
        own_ref[begin : begin + size, :] = value

    def store_u(begin, size, value):
        u_ref[begin : begin + size, :] = value

    advance(tiles, GROUPS_OF_TILES, *fields, coarse_rhs, COARSE_C, COARSE_R, COARSE_Q, walls, store_own)

    def step(_, carry):
        advance(tiles, GROUPS_OF_TILES, *fields, fine_rhs, FINE_C, FINE_R, 1.0, walls, store_u)
        return carry

    lax.fori_loop(0, STEPS, step, 0, unroll=4)
    for t in range(tiles):
        rows = slice(8 * t, 8 * t + 8)
        value = u_ref[rows, :]
        value = jnp.where(group == 0, value, value - own_ref[rows, :])
        own_ref[rows, :] = value
        plain_u[pl.ds(t, 8, stride=tiles), :] = value
    for k in range(parts):
        first = pl.multiple_of(placed(second, k, parts) * each + (HALO - reach), CELL_BLOCK)
        windows_ref[k] = plain_u[pl.ds(first, WINDOW), :]


def fine_phase(parts, ends, low, high, start, heat, base, fine_rhs, coarse_rhs):
    total = start.shape[0] + 2 * HALO
    operands = (low, high, start, heat, base, fine_rhs, coarse_rhs)
    field = jax.ShapeDtypeStruct((total, NY), jnp.float32)
    window = jax.ShapeDtypeStruct((WINDOW, NY), jnp.float32)
    return pl.pallas_call(
        functools.partial(fine_kernel, ends),
        out_shape=(jax.ShapeDtypeStruct((parts, WINDOW, NY), jnp.float32), field, field, field, window, window),
        in_specs=[whole(x.shape) for x in operands],
        out_specs=(whole((parts, WINDOW, NY)), *[whole(field.shape)] * 3, *[whole(window.shape)] * 2),
        scratch_shapes=[pltpu.VMEM((total, NY), jnp.float32)] * 7,
        compiler_params=pltpu.CompilerParams(vmem_limit_bytes=VMEM_LIMIT),
        name="fine_phase",
    )(*operands)


def sweep_window(ends, jumps_ref, base_window_ref, source_window_ref, rhs, back_ref, begin_ref, first, last, scratch):
    u_ref, base_ref, source_ref, still_ref, slope_ref, w_ref, plain = scratch
    parts = jumps_ref.shape[0]
    space, group = lax.axis_index("space"), lax.axis_index("tm")
    tiles = WINDOW // 8
    for t in range(tiles):
        rows = slice(8 * t, 8 * t + 8)
        u_ref[rows, :] = begin_ref[pl.ds(t, 8, stride=tiles), :]
        base_ref[rows, :] = base_window_ref[pl.ds(t, 8, stride=tiles), :]
        source_ref[rows, :] = source_window_ref[pl.ds(t, 8, stride=tiles), :]
    back_ref[first] = begin_ref[MARGIN : MARGIN + BACK, :]
    side = HALO - CELL_BLOCK
    each = WINDOW - 2 * side
    second = group >= parts
    window = placed(second, jnp.where(second, group - parts, group), parts)
    under, over = divmod(side - 1, tiles), divmod(side + each, tiles)
    walls = [
        (under[1], wall((space == 0) & (window == 0), under[0])),
        (over[1], wall((space == ends) & (window == parts - 1), over[0])),
    ]
    fields = (u_ref, base_ref, source_ref, still_ref, slope_ref, w_ref)

    def turn(g, carry):
        def store(begin, size, value):
            for n in range(size // 8):
                t = begin // 8 + n
                moved = value[8 * n : 8 * n + 8] + jumps_ref[g, pl.ds(t, 8, stride=tiles), :]
                u_ref[8 * t : 8 * t + 8, :] = moved
                plain[pl.ds(t, 8, stride=tiles), :] = moved

        advance(tiles, SWEEP_GROUPS_OF_TILES, *fields, rhs, COARSE_C, COARSE_R, COARSE_Q, walls, store)

        @pl.when(g + 1 < parts)
        def _():
            back_ref[g + 1] = plain[MARGIN : MARGIN + BACK, :]

        return carry

    lax.fori_loop(first, last, turn, 0)


def first_sweep_kernel(ends, jumps_ref, base_window_ref, source_window_ref, rhs, back_ref, over_ref, *scratch):
    parts = jumps_ref.shape[0]

    @pl.when(lax.axis_index("tm") < parts)
    def _():
        back_ref[0] = jnp.zeros((BACK, NY), jnp.float32)
        windows = (jumps_ref, base_window_ref, source_window_ref, rhs)
        sweep_window(ends, *windows, back_ref, jumps_ref.at[0], 1, parts, scratch)
        over_ref[...] = scratch[-1][...]


def second_sweep_kernel(ends, jumps_ref, base_window_ref, source_window_ref, rhs, first_ref, over_ref, back_ref, *scratch):
    parts = jumps_ref.shape[0]
    second = lax.axis_index("tm") >= parts

    @pl.when(jnp.logical_not(second))
    def _():
        back_ref[...] = first_ref[...]

    @pl.when(second)
    def _():
        windows = (jumps_ref, base_window_ref, source_window_ref, rhs)
        sweep_window(ends, *windows, back_ref, over_ref, 0, parts - 1, scratch)


def sweep(kernel, ends, outputs, *operands):
    window = pltpu.VMEM((WINDOW, NY), jnp.float32)
    return pl.pallas_call(
        functools.partial(kernel, ends),
        out_shape=tuple(jax.ShapeDtypeStruct(shape, jnp.float32) for shape in outputs),
        in_specs=[whole(x.shape) for x in operands],
        out_specs=tuple(whole(shape) for shape in outputs),
        scratch_shapes=[window] * 7,
        compiler_params=pltpu.CompilerParams(vmem_limit_bytes=VMEM_LIMIT),
        name="sweep",
    )(*operands)


def last_kernel(
    ends, parts_ref, own_ref, base_ref, source_ref, start_ref, rhs, ends_ref, next_ref, plain, u_ref, still_ref, slope_ref, w_ref
):
    space, group = lax.axis_index("space"), lax.axis_index("tm")
    parts = parts_ref.shape[0]
    slab = next_ref.shape[0]
    total = slab + 2 * HALO
    tiles = total // 8
    each = slab // parts
    side = (BACK - each) // 2
    empty = jnp.zeros((HALO - 8, NY), jnp.float32)
    plain[0 : HALO - 8, :] = empty
    plain[total - HALO + 8 :, :] = empty
    gap = jnp.zeros((8 - side, NY), jnp.float32)
    second = group >= parts
    lowest = parts_ref[placed(second, 0, parts), 0:side, :]
    highest = parts_ref[placed(second, parts - 1, parts), BACK - side : BACK, :]
    plain[HALO - 8 : HALO, :] = jnp.concatenate([gap, lowest], axis=0)
    plain[HALO + slab : HALO + slab + 8, :] = jnp.concatenate([highest, gap], axis=0)
    for k in range(parts):
        value = parts_ref[placed(second, k, parts), side : side + each, :]
        plain[HALO + each * k : HALO + each * (k + 1), :] = value
        rows = slice(each * k, each * (k + 1))
        next_ref[rows, :] = jnp.where(group == 0, start_ref[rows, :], value)
    for t in range(tiles):
        u_ref[8 * t : 8 * t + 8, :] = plain[pl.ds(t, 8, stride=tiles), :]
    under, over = divmod(HALO - 1, tiles), divmod(HALO + slab, tiles)
    walls = [(under[1], wall(space == 0, under[0])), (over[1], wall(space == ends, over[0]))]

    def store(begin, size, value):
        for n in range(size // 8):
            t = begin // 8 + n
            own = own_ref[8 * t : 8 * t + 8, :]
            moved = value[8 * n : 8 * n + 8]
            plain[pl.ds(t, 8, stride=tiles), :] = jnp.where(group == 0, own, moved + own)

    fields = (u_ref, base_ref, source_ref, still_ref, slope_ref, w_ref)
    advance(tiles, GROUPS_OF_TILES, *fields, rhs, COARSE_C, COARSE_R, COARSE_Q, walls, store)
    ends_ref[...] = plain[HALO : HALO + slab, :]


def last_step(ends, back, own, base, source, start, coarse_rhs):
    field = jax.ShapeDtypeStruct(start.shape, jnp.float32)
    total = own.shape
    return pl.pallas_call(
        functools.partial(last_kernel, ends),
        out_shape=(field, field),
        in_specs=[whole(back.shape), whole(total), whole(total), whole(total), whole(start.shape), whole(coarse_rhs.shape)],
        out_specs=(whole(start.shape), whole(start.shape)),
        scratch_shapes=[pltpu.VMEM(total, jnp.float32)] * 5,
        compiler_params=pltpu.CompilerParams(vmem_limit_bytes=VMEM_LIMIT),
        name="last_step",
    )(back, own, base, source, start, coarse_rhs)


def on_device(starts, region, viscosity, heat_source, fine_line, coarse_line):
    start = starts[0]
    groups = lax.axis_size("tm")
    parts = groups // BLOCKS
    members = [list(range(parts)), list(range(parts, groups))]
    ends = lax.axis_size("space") - 1
    head, tail = pack(*stay(viscosity, region.T, start, heat_source))
    low = lax.ppermute(tail, "space", [(i, i + 1) for i in range(ends)])
    high = lax.ppermute(head, "space", [(i + 1, i) for i in range(ends)])
    fine_rhs, coarse_rhs, middle = stage(*stay(viscosity, region.T, fine_line, coarse_line))
    windows, own, base, source, base_window, source_window = fine_phase(
        parts, ends, low, high, start, heat_source, middle, fine_rhs, coarse_rhs
    )
    jumps = lax.all_to_all(windows, "tm", 0, 0, axis_index_groups=members)
    back_shape = (parts, BACK, NY)
    given = (jumps, base_window, source_window, coarse_rhs)
    first_back, over = sweep(first_sweep_kernel, ends, (back_shape, (WINDOW, NY)), *given)
    over = lax.ppermute(over, "tm", [(k, parts + mirrored(k, parts)) for k in range(parts)])
    (back,) = sweep(second_sweep_kernel, ends, (back_shape,), *given, first_back, over)
    mine = lax.all_to_all(back, "tm", 0, 0, axis_index_groups=members)
    value, following = last_step(ends, mine, own, base, source, start, coarse_rhs)
    return value[None], following[None]


def solution(mesh):
    placed = (P("tm", "space", None), P("space", None), P(), P("space", None), P(), P())
    return jax.shard_map(
        on_device,
        mesh=mesh,
        in_specs=placed,
        out_specs=(P("tm", "space", None), P("tm", "space", None)),
        check_vma=False,
    )
```

```python
import functools

import jax
import jax.numpy as jnp
from jax import lax
from jax.experimental import pallas as pl
from jax.experimental.pallas import tpu as pltpu
from jax.sharding import PartitionSpec as P

NY = 128
CELL_BLOCK = 16
REGIONS = 8
STEPS = 8

FINE_C = 0.3
FINE_R = 0.2
COARSE_C = 0.5
COARSE_R = 0.12
COARSE_Q = 3.0

HALO = 48
HALO_BLOCKS = HALO // CELL_BLOCK
PACK = 2 * HALO + 8
WINDOW = 192
MARGIN = 28
BACK = WINDOW - 2 * MARGIN
BLOCKS = 2
GROUPS_OF_TILES = 6
SWEEP_GROUPS_OF_TILES = 2
VMEM_LIMIT = 16 * 1024 * 1024
SMALL_VMEM_LIMIT = 4 * 1024 * 1024


def from_left(tile):
    return pltpu.roll(tile, 1, 0)


def from_right(tile):
    return pltpu.roll(tile, 7, 0)


def halves(x):
    high = x.astype(jnp.bfloat16)
    low = (x - high.astype(jnp.float32)).astype(jnp.bfloat16)
    return high, low


def line_operand(line_ref):
    high, low = halves(line_ref[...].T)
    top = jnp.concatenate([high, low], axis=1)
    return jnp.concatenate([top, top], axis=0)


def product(pairs, rhs_ref):
    left = jnp.concatenate([jnp.concatenate(halves(e), axis=1) for e in pairs], axis=0)
    both = jnp.dot(left, rhs_ref[...], preferred_element_type=jnp.float32)
    return both[:, :NY] + both[:, NY:]


def rotated(pairs, count, turn):
    cuts = [pairs * n // count for n in range(count + 1)]
    groups = [list(range(cuts[n], cuts[n + 1])) for n in range(count)]
    return groups[turn:] + groups[:turn]


def flux_pass(groups, viscosity_of, slope_of, base_of, walls, rhs_ref, store):
    order = [i for group in groups for i in group]
    pairs = len(order)
    begin, prior = order[0], order[-1]
    m_begin = m = viscosity_of(begin)
    top = m[:8]
    if begin == 0:
        top = from_right(top)
    before = (viscosity_of(prior)[8:] + top) * slope_of(prior)[8:]
    if begin == 0:
        before = from_left(before)
    n = 0
    for group in groups:
        done = []
        for i in group:
            n += 1
            following = m_begin if n == pairs else viscosity_of(order[n])
            top = following[:8]
            if i + 1 == pairs:
                top = from_right(top)
            flux = (m + jnp.concatenate([m[8:], top], axis=0)) * slope_of(i)
            e = base_of(i) + (flux - jnp.concatenate([before, flux[:8]], axis=0))
            for tile, mask in walls:
                if tile // 2 == i:
                    ones = jnp.ones_like(mask)
                    both = [mask, ones] if tile % 2 == 0 else [ones, mask]
                    e = e * jnp.concatenate(both, axis=0)
            before = flux[8:]
            if i + 1 == pairs:
                before = from_left(before)
            m = following
            done.append(e)
        store(16 * group[0], 16 * len(group), product(done, rhs_ref))


def advance(tiles, parts, u_ref, base_ref, heat_ref, still_ref, slope_ref, w_ref, rhs_ref, courant, ratio, weight, walls, store):
    pairs = tiles // 2

    def rows(i):
        return slice(16 * i, 16 * i + 16)

    def viscosity_first(i):
        u = u_ref[rows(i), :]
        return base_ref[rows(i), :] / (2.0 + u * u)

    def viscosity_second(i):
        u = 0.5 * (u_ref[rows(i), :] + w_ref[rows(i), :])
        return base_ref[rows(i), :] / (2.0 + u * u)

    right = from_right(u_ref[0:8, :])

    def step_up(i):
        u = u_ref[rows(i), :]
        if i + 1 < pairs:
            above = u_ref[16 * i + 8 : 16 * i + 24, :]
        else:
            above = jnp.concatenate([u[8:], right], axis=0)
        return above - u

    def slope_first(i):
        return ratio * step_up(i)

    def still_first(i):
        up = step_up(i)
        slope_ref[rows(i), :] = ratio * up
        prior = from_left(step_up(pairs - 1)[8:]) if i == 0 else step_up(i - 1)[8:]
        heat = heat_ref[rows(i), :]
        if weight != 1.0:
            heat = weight * heat
        still = (u_ref[rows(i), :] + heat) - courant * jnp.concatenate([prior, up[:8]], axis=0)
        still_ref[rows(i), :] = still
        return still

    def store_first(start, count, value):
        w_ref[start : start + count, :] = value

    flux_pass(rotated(pairs, parts, 0), viscosity_first, slope_first, still_first, walls, rhs_ref, store_first)
    flux_pass(
        rotated(pairs, parts, parts // 2),
        viscosity_second,
        lambda i: slope_ref[rows(i), :],
        lambda i: still_ref[rows(i), :],
        walls,
        rhs_ref,
        store,
    )


def wall(at_wall, sublane):
    row = lax.broadcasted_iota(jnp.int32, (8, NY), 0)
    return jnp.where((row == sublane) & at_wall, 0.0, 1.0)


def mirrored(part, parts):
    return (parts // 2 - 1 - part // 2) * 2 + part % 2


def placed(second, part, parts):
    return jnp.where(second, mirrored(part, parts), part)


def whole(shape):
    return pl.BlockSpec(shape, lambda: (0,) * len(shape))


ANYWHERE = pl.BlockSpec(memory_space=pl.ANY)


def spread_blocks(viscosity_ref, region_ref):
    region = region_ref[...]
    count = region.shape[1]
    picked = jnp.zeros(region.shape, jnp.float32)
    for value in range(REGIONS):
        picked = jnp.where(region == value, viscosity_ref[value], picked)
    wide = jnp.concatenate([picked, jnp.zeros((region.shape[0], NY - count), jnp.float32)], axis=1)
    cells = [jnp.broadcast_to(wide[n : n + 1], (CELL_BLOCK, NY)) for n in range(NY // CELL_BLOCK)]
    return jnp.concatenate(cells, axis=0).T[:count]


def stay(*arrays):
    return [pltpu.with_memory_space_constraint(x, pltpu.HBM) for x in arrays]


def pack_kernel(viscosity_ref, region_ref, start_ref, heat_ref, outer_ref, inner_ref, sems):
    slab = start_ref.shape[0]
    odd = lax.axis_index("space") % 2
    copies = []
    for n, (edge, last) in enumerate(((outer_ref, odd), (inner_ref, 1 - odd))):
        first = pl.multiple_of(last * (slab - HALO), CELL_BLOCK)
        for m, field in enumerate((start_ref, heat_ref)):
            target = edge.at[pl.ds(m * HALO, HALO)]
            copies.append(pltpu.make_async_copy(field.at[pl.ds(first, HALO)], target, sems.at[2 * n + m]))
    for copy in copies:
        copy.start()
    spread = spread_blocks(viscosity_ref, region_ref)
    head, tail = spread[:8], spread[spread.shape[0] - 8 :]
    outer_ref[2 * HALO :, :] = jnp.where(odd == 1, tail, head)
    inner_ref[2 * HALO :, :] = jnp.where(odd == 1, head, tail)
    for copy in copies:
        copy.wait()


def pack(viscosity, region, start, heat):
    edge = (PACK, NY)
    return pl.pallas_call(
        pack_kernel,
        out_shape=(jax.ShapeDtypeStruct(edge, jnp.float32), jax.ShapeDtypeStruct(edge, jnp.float32)),
        in_specs=[pl.BlockSpec(memory_space=pltpu.SMEM), whole(region.shape), ANYWHERE, ANYWHERE],
        out_specs=(whole(edge), whole(edge)),
        scratch_shapes=[pltpu.SemaphoreType.DMA((4,))],
        compiler_params=pltpu.CompilerParams(vmem_limit_bytes=SMALL_VMEM_LIMIT),
        name="pack",
    )(viscosity, region, start, heat)


def stage_kernel(viscosity_ref, region_ref, fine_ref, coarse_ref, fine_rhs, coarse_rhs, base_ref):
    spread = spread_blocks(viscosity_ref, region_ref)
    for b in range(spread.shape[0]):
        base_ref[CELL_BLOCK * b : CELL_BLOCK * (b + 1), :] = jnp.broadcast_to(spread[b : b + 1], (CELL_BLOCK, NY))
    fine_rhs[...] = line_operand(fine_ref)
    coarse_rhs[...] = line_operand(coarse_ref)


def stage(viscosity, region, fine_line, coarse_line):
    rows = region.shape[1] * CELL_BLOCK
    square = (2 * NY, 2 * NY)
    return pl.pallas_call(
        stage_kernel,
        out_shape=(
            jax.ShapeDtypeStruct(square, jnp.bfloat16),
            jax.ShapeDtypeStruct(square, jnp.bfloat16),
            jax.ShapeDtypeStruct((rows, NY), jnp.float32),
        ),
        in_specs=[pl.BlockSpec(memory_space=pltpu.SMEM), whole(region.shape), whole((NY, NY)), whole((NY, NY))],
        out_specs=(whole(square), whole(square), whole((rows, NY))),
        compiler_params=pltpu.CompilerParams(vmem_limit_bytes=SMALL_VMEM_LIMIT),
        cost_estimate=pl.CostEstimate(flops=rows * NY, bytes_accessed=8 * rows * NY, transcendentals=0),
        name="stage",
    )(viscosity, region, fine_line, coarse_line)


def fine_kernel(
    ends,
    outer_ref,
    inner_ref,
    start_ref,
    heat_ref,
    middle_ref,
    fine_rhs,
    coarse_rhs,
    windows_ref,
    own_ref,
    base_ref,
    source_ref,
    base_window_ref,
    source_window_ref,
    plain_u,
    plain_q,
    plain_m,
    u_ref,
    still_ref,
    slope_ref,
    w_ref,
):
    space, group = lax.axis_index("space"), lax.axis_index("tm")
    slab = start_ref.shape[0]
    total = slab + 2 * HALO
    tiles = total // 8
    odd = space % 2 == 1

    def low(rows):
        return jnp.where(odd, inner_ref[rows, :], outer_ref[rows, :])

    def high(rows):
        return jnp.where(odd, outer_ref[rows, :], inner_ref[rows, :])

    for plain, part, middle in ((plain_u, 0, start_ref), (plain_q, HALO, heat_ref)):
        plain[0:HALO, :] = low(slice(part, part + HALO))
        plain[HALO : HALO + slab, :] = middle[...]
        plain[HALO + slab :, :] = high(slice(part, part + HALO))
    plain_m[HALO : HALO + slab, :] = middle_ref[...]
    low_blocks, high_blocks = low(slice(2 * HALO, PACK)), high(slice(2 * HALO, PACK))
    for b in range(HALO_BLOCKS):
        n = 8 - HALO_BLOCKS + b
        rows = slice(CELL_BLOCK * b, CELL_BLOCK * (b + 1))
        plain_m[rows, :] = jnp.broadcast_to(low_blocks[n : n + 1, :], (CELL_BLOCK, NY))
        rows = slice(HALO + slab + CELL_BLOCK * b, HALO + slab + CELL_BLOCK * (b + 1))
        plain_m[rows, :] = jnp.broadcast_to(high_blocks[b : b + 1, :], (CELL_BLOCK, NY))
    parts = windows_ref.shape[0]
    each = slab // parts
    reach = (WINDOW - each) // 2
    second = group >= parts
    place = jnp.where(second, group - parts, group)
    corner = pl.multiple_of(placed(second, place, parts) * each + (HALO - reach), CELL_BLOCK)
    base_window_ref[...] = plain_m[pl.ds(corner, WINDOW), :]
    source_window_ref[...] = plain_q[pl.ds(corner, WINDOW), :]
    for plain, ref in ((plain_u, u_ref), (plain_q, source_ref), (plain_m, base_ref)):
        for t in range(tiles):
            ref[8 * t : 8 * t + 8, :] = plain[pl.ds(t, 8, stride=tiles), :]

    under, over = divmod(HALO - 1, tiles), divmod(HALO + slab, tiles)
    walls = [(under[1], wall(space == 0, under[0])), (over[1], wall(space == ends, over[0]))]
    fields = (u_ref, base_ref, source_ref, still_ref, slope_ref, w_ref)

    def store_own(begin, size, value):
        own_ref[begin : begin + size, :] = value

    def store_u(begin, size, value):
        u_ref[begin : begin + size, :] = value

    advance(tiles, GROUPS_OF_TILES, *fields, coarse_rhs, COARSE_C, COARSE_R, COARSE_Q, walls, store_own)

    def step(_, carry):
        advance(tiles, GROUPS_OF_TILES, *fields, fine_rhs, FINE_C, FINE_R, 1.0, walls, store_u)
        return carry

    lax.fori_loop(0, STEPS, step, 0, unroll=4)
    for t in range(tiles):
        rows = slice(8 * t, 8 * t + 8)
        value = u_ref[rows, :]
        value = jnp.where(group == 0, value, value - own_ref[rows, :])
        own_ref[rows, :] = value
        plain_u[pl.ds(t, 8, stride=tiles), :] = value
    for k in range(parts):
        first = pl.multiple_of(placed(second, k, parts) * each + (HALO - reach), CELL_BLOCK)
        windows_ref[k] = plain_u[pl.ds(first, WINDOW), :]


def fine_phase(parts, ends, outer, inner, start, heat, base, fine_rhs, coarse_rhs):
    total = start.shape[0] + 2 * HALO
    operands = (outer, inner, start, heat, base, fine_rhs, coarse_rhs)
    field = jax.ShapeDtypeStruct((total, NY), jnp.float32)
    window = jax.ShapeDtypeStruct((WINDOW, NY), jnp.float32)
    return pl.pallas_call(
        functools.partial(fine_kernel, ends),
        out_shape=(jax.ShapeDtypeStruct((parts, WINDOW, NY), jnp.float32), field, field, field, window, window),
        in_specs=[whole(x.shape) for x in operands],
        out_specs=(whole((parts, WINDOW, NY)), *[whole(field.shape)] * 3, *[whole(window.shape)] * 2),
        scratch_shapes=[pltpu.VMEM((total, NY), jnp.float32)] * 7,
        compiler_params=pltpu.CompilerParams(vmem_limit_bytes=VMEM_LIMIT),
        name="fine_phase",
    )(*operands)


def sweep_window(ends, jumps_ref, base_window_ref, source_window_ref, rhs, back_ref, begin_ref, first, last, scratch):
    u_ref, base_ref, source_ref, still_ref, slope_ref, w_ref, plain = scratch
    parts = jumps_ref.shape[0]
    space, group = lax.axis_index("space"), lax.axis_index("tm")
    tiles = WINDOW // 8
    for t in range(tiles):
        rows = slice(8 * t, 8 * t + 8)
        u_ref[rows, :] = begin_ref[pl.ds(t, 8, stride=tiles), :]
        base_ref[rows, :] = base_window_ref[pl.ds(t, 8, stride=tiles), :]
        source_ref[rows, :] = source_window_ref[pl.ds(t, 8, stride=tiles), :]
    back_ref[first] = begin_ref[MARGIN : MARGIN + BACK, :]
    side = HALO - CELL_BLOCK
    each = WINDOW - 2 * side
    second = group >= parts
    window = placed(second, jnp.where(second, group - parts, group), parts)
    under, over = divmod(side - 1, tiles), divmod(side + each, tiles)
    walls = [
        (under[1], wall((space == 0) & (window == 0), under[0])),
        (over[1], wall((space == ends) & (window == parts - 1), over[0])),
    ]
    fields = (u_ref, base_ref, source_ref, still_ref, slope_ref, w_ref)

    def turn(g, carry):
        def store(begin, size, value):
            for n in range(size // 8):
                t = begin // 8 + n
                moved = value[8 * n : 8 * n + 8] + jumps_ref[g, pl.ds(t, 8, stride=tiles), :]
                u_ref[8 * t : 8 * t + 8, :] = moved
                plain[pl.ds(t, 8, stride=tiles), :] = moved

        advance(tiles, SWEEP_GROUPS_OF_TILES, *fields, rhs, COARSE_C, COARSE_R, COARSE_Q, walls, store)

        @pl.when(g + 1 < parts)
        def _():
            back_ref[g + 1] = plain[MARGIN : MARGIN + BACK, :]

        return carry

    lax.fori_loop(first, last, turn, 0)


def first_sweep_kernel(ends, jumps_ref, base_window_ref, source_window_ref, rhs, back_ref, over_ref, *scratch):
    parts = jumps_ref.shape[0]

    @pl.when(lax.axis_index("tm") < parts)
    def _():
        back_ref[0] = jnp.zeros((BACK, NY), jnp.float32)
        windows = (jumps_ref, base_window_ref, source_window_ref, rhs)
        sweep_window(ends, *windows, back_ref, jumps_ref.at[0], 1, parts, scratch)
        over_ref[...] = scratch[-1][...]


def second_sweep_kernel(ends, jumps_ref, base_window_ref, source_window_ref, rhs, first_ref, over_ref, back_ref, *scratch):
    parts = jumps_ref.shape[0]
    second = lax.axis_index("tm") >= parts

    @pl.when(jnp.logical_not(second))
    def _():
        back_ref[...] = first_ref[...]

    @pl.when(second)
    def _():
        windows = (jumps_ref, base_window_ref, source_window_ref, rhs)
        sweep_window(ends, *windows, back_ref, over_ref, 0, parts - 1, scratch)


def sweep(kernel, ends, outputs, *operands):
    window = pltpu.VMEM((WINDOW, NY), jnp.float32)
    return pl.pallas_call(
        functools.partial(kernel, ends),
        out_shape=tuple(jax.ShapeDtypeStruct(shape, jnp.float32) for shape in outputs),
        in_specs=[whole(x.shape) for x in operands],
        out_specs=tuple(whole(shape) for shape in outputs),
        scratch_shapes=[window] * 7,
        compiler_params=pltpu.CompilerParams(vmem_limit_bytes=VMEM_LIMIT),
        name="sweep",
    )(*operands)


def last_kernel(
    ends, parts_ref, own_ref, base_ref, source_ref, start_ref, rhs, ends_ref, next_ref, plain, u_ref, still_ref, slope_ref, w_ref
):
    space, group = lax.axis_index("space"), lax.axis_index("tm")
    parts = parts_ref.shape[0]
    slab = next_ref.shape[0]
    total = slab + 2 * HALO
    tiles = total // 8
    each = slab // parts
    side = (BACK - each) // 2
    empty = jnp.zeros((HALO - 8, NY), jnp.float32)
    plain[0 : HALO - 8, :] = empty
    plain[total - HALO + 8 :, :] = empty
    gap = jnp.zeros((8 - side, NY), jnp.float32)
    second = group >= parts
    lowest = parts_ref[placed(second, 0, parts), 0:side, :]
    highest = parts_ref[placed(second, parts - 1, parts), BACK - side : BACK, :]
    plain[HALO - 8 : HALO, :] = jnp.concatenate([gap, lowest], axis=0)
    plain[HALO + slab : HALO + slab + 8, :] = jnp.concatenate([highest, gap], axis=0)
    for k in range(parts):
        value = parts_ref[placed(second, k, parts), side : side + each, :]
        plain[HALO + each * k : HALO + each * (k + 1), :] = value
        rows = slice(each * k, each * (k + 1))
        next_ref[rows, :] = jnp.where(group == 0, start_ref[rows, :], value)
    for t in range(tiles):
        u_ref[8 * t : 8 * t + 8, :] = plain[pl.ds(t, 8, stride=tiles), :]
    under, over = divmod(HALO - 1, tiles), divmod(HALO + slab, tiles)
    walls = [(under[1], wall(space == 0, under[0])), (over[1], wall(space == ends, over[0]))]

    def store(begin, size, value):
        for n in range(size // 8):
            t = begin // 8 + n
            own = own_ref[8 * t : 8 * t + 8, :]
            moved = value[8 * n : 8 * n + 8]
            plain[pl.ds(t, 8, stride=tiles), :] = jnp.where(group == 0, own, moved + own)

    fields = (u_ref, base_ref, source_ref, still_ref, slope_ref, w_ref)
    advance(tiles, GROUPS_OF_TILES, *fields, rhs, COARSE_C, COARSE_R, COARSE_Q, walls, store)
    ends_ref[...] = plain[HALO : HALO + slab, :]


def last_step(ends, back, own, base, source, start, coarse_rhs):
    field = jax.ShapeDtypeStruct(start.shape, jnp.float32)
    total = own.shape
    return pl.pallas_call(
        functools.partial(last_kernel, ends),
        out_shape=(field, field),
        in_specs=[whole(back.shape), whole(total), whole(total), whole(total), whole(start.shape), whole(coarse_rhs.shape)],
        out_specs=(whole(start.shape), whole(start.shape)),
        scratch_shapes=[pltpu.VMEM(total, jnp.float32)] * 5,
        compiler_params=pltpu.CompilerParams(vmem_limit_bytes=VMEM_LIMIT),
        name="last_step",
    )(back, own, base, source, start, coarse_rhs)


def on_device(starts, region, viscosity, heat_source, fine_line, coarse_line):
    start = starts[0]
    groups = lax.axis_size("tm")
    parts = groups // BLOCKS
    members = [list(range(parts)), list(range(parts, groups))]
    ends = lax.axis_size("space") - 1
    outer, inner = pack(*stay(viscosity, region.T, start, heat_source))
    apart = [(i, i + 1) for i in range(1, ends, 2)]
    within = [(i, i + 1) for i in range(0, ends, 2)]
    outer, inner = (lax.ppermute(x, "space", pairs + [(j, i) for i, j in pairs]) for x, pairs in ((outer, apart), (inner, within)))
    fine_rhs, coarse_rhs, middle = stage(*stay(viscosity, region.T, fine_line, coarse_line))
    windows, own, base, source, base_window, source_window = fine_phase(
        parts, ends, outer, inner, start, heat_source, middle, fine_rhs, coarse_rhs
    )
    jumps = lax.all_to_all(windows, "tm", 0, 0, axis_index_groups=members)
    back_shape = (parts, BACK, NY)
    given = (jumps, base_window, source_window, coarse_rhs)
    first_back, over = sweep(first_sweep_kernel, ends, (back_shape, (WINDOW, NY)), *given)
    over = lax.ppermute(over, "tm", [(k, parts + mirrored(k, parts)) for k in range(parts)])
    (back,) = sweep(second_sweep_kernel, ends, (back_shape,), *given, first_back, over)
    mine = lax.all_to_all(back, "tm", 0, 0, axis_index_groups=members)
    value, following = last_step(ends, mine, own, base, source, start, coarse_rhs)
    return value[None], following[None]


def solution(mesh):
    placed = (P("tm", "space", None), P("space", None), P(), P("space", None), P(), P())
    return jax.shard_map(
        on_device,
        mesh=mesh,
        in_specs=placed,
        out_specs=(P("tm", "space", None), P("tm", "space", None)),
        check_vma=False,
    )
```

```python
import functools

import jax
import jax.numpy as jnp
from jax import lax
from jax.experimental import pallas as pl
from jax.experimental.pallas import tpu as pltpu
from jax.sharding import PartitionSpec as P

NY = 128
CELL_BLOCK = 16
REGIONS = 8
STEPS = 8

FINE_C = 0.3
FINE_R = 0.2
COARSE_C = 0.5
COARSE_R = 0.12
COARSE_Q = 3.0

HALO = 48
HALO_BLOCKS = HALO // CELL_BLOCK
PACK = 2 * HALO + 8
WINDOW = 192
MARGIN = 28
BACK = WINDOW - 2 * MARGIN
OVER = WINDOW - 16
BLOCKS = 2
GROUPS_OF_TILES = 6
SWEEP_GROUPS_OF_TILES = 2
VMEM_LIMIT = 16 * 1024 * 1024
SMALL_VMEM_LIMIT = 4 * 1024 * 1024


def from_left(tile):
    return pltpu.roll(tile, 1, 0)


def from_right(tile):
    return pltpu.roll(tile, 7, 0)


def halves(x):
    high = x.astype(jnp.bfloat16)
    low = (x - high.astype(jnp.float32)).astype(jnp.bfloat16)
    return high, low


def line_operand(line_ref):
    high, low = halves(line_ref[...].T)
    top = jnp.concatenate([high, low], axis=1)
    return jnp.concatenate([top, top], axis=0)


def product(pairs, rhs_ref):
    left = jnp.concatenate([jnp.concatenate(halves(e), axis=1) for e in pairs], axis=0)
    both = jnp.dot(left, rhs_ref[...], preferred_element_type=jnp.float32)
    return both[:, :NY] + both[:, NY:]


def rotated(pairs, count, turn):
    cuts = [pairs * n // count for n in range(count + 1)]
    groups = [list(range(cuts[n], cuts[n + 1])) for n in range(count)]
    return groups[turn:] + groups[:turn]


def flux_pass(groups, viscosity_of, slope_of, base_of, walls, rhs_ref, store):
    order = [i for group in groups for i in group]
    pairs = len(order)
    begin, prior = order[0], order[-1]
    m_begin = m = viscosity_of(begin)
    top = m[:8]
    if begin == 0:
        top = from_right(top)
    before = (viscosity_of(prior)[8:] + top) * slope_of(prior)[8:]
    if begin == 0:
        before = from_left(before)
    n = 0
    for group in groups:
        done = []
        for i in group:
            n += 1
            following = m_begin if n == pairs else viscosity_of(order[n])
            top = following[:8]
            if i + 1 == pairs:
                top = from_right(top)
            flux = (m + jnp.concatenate([m[8:], top], axis=0)) * slope_of(i)
            e = base_of(i) + (flux - jnp.concatenate([before, flux[:8]], axis=0))
            for tile, mask in walls:
                if tile // 2 == i:
                    ones = jnp.ones_like(mask)
                    both = [mask, ones] if tile % 2 == 0 else [ones, mask]
                    e = e * jnp.concatenate(both, axis=0)
            before = flux[8:]
            if i + 1 == pairs:
                before = from_left(before)
            m = following
            done.append(e)
        store(16 * group[0], 16 * len(group), product(done, rhs_ref))


def recent(compute, count):
    kept = {}

    def call(i):
        if i in kept:
            kept[i] = kept.pop(i)
        else:
            kept[i] = compute(i)
            if len(kept) > count:
                del kept[next(iter(kept))]
        return kept[i]

    return call


def advance(tiles, parts, u_ref, base_ref, heat_ref, still_ref, slope_ref, w_ref, rhs_ref, courant, ratio, weight, walls, store):
    pairs = tiles // 2

    def rows(i):
        return slice(16 * i, 16 * i + 16)

    u_at = recent(lambda i: u_ref[rows(i), :], 3)

    def viscosity_first(i):
        u = u_at(i)
        return base_ref[rows(i), :] / (2.0 + u * u)

    def viscosity_second(i):
        u = 0.5 * (u_ref[rows(i), :] + w_ref[rows(i), :])
        return base_ref[rows(i), :] / (2.0 + u * u)

    right = from_right(u_ref[0:8, :])

    def step(i):
        u = u_at(i)
        top = u_at(i + 1)[:8] if i + 1 < pairs else right
        return jnp.concatenate([u[8:], top], axis=0) - u

    step_up = recent(step, 2)

    def slope_first(i):
        return ratio * step_up(i)

    def still_first(i):
        up = step_up(i)
        slope_ref[rows(i), :] = ratio * up
        prior = from_left(step_up(pairs - 1)[8:]) if i == 0 else step_up(i - 1)[8:]
        heat = heat_ref[rows(i), :]
        if weight != 1.0:
            heat = weight * heat
        still = (u_at(i) + heat) - courant * jnp.concatenate([prior, up[:8]], axis=0)
        still_ref[rows(i), :] = still
        return still

    def store_first(start, count, value):
        w_ref[start : start + count, :] = value

    flux_pass(rotated(pairs, parts, 0), viscosity_first, slope_first, still_first, walls, rhs_ref, store_first)
    flux_pass(
        rotated(pairs, parts, parts // 2),
        viscosity_second,
        lambda i: slope_ref[rows(i), :],
        lambda i: still_ref[rows(i), :],
        walls,
        rhs_ref,
        store,
    )


def wall(at_wall, sublane):
    row = lax.broadcasted_iota(jnp.int32, (8, NY), 0)
    return jnp.where((row == sublane) & at_wall, 0.0, 1.0)


def mirrored(part, parts):
    return (parts // 2 - 1 - part // 2) * 2 + part % 2


def placed(second, part, parts):
    return jnp.where(second, mirrored(part, parts), part)


def whole(shape):
    return pl.BlockSpec(shape, lambda: (0,) * len(shape))


ANYWHERE = pl.BlockSpec(memory_space=pl.ANY)


def spread_blocks(viscosity_ref, region_ref):
    region = region_ref[...]
    count = region.shape[1]
    picked = jnp.zeros(region.shape, jnp.float32)
    for value in range(REGIONS):
        picked = jnp.where(region == value, viscosity_ref[value], picked)
    wide = jnp.concatenate([picked, jnp.zeros((region.shape[0], NY - count), jnp.float32)], axis=1)
    cells = [jnp.broadcast_to(wide[n : n + 1], (CELL_BLOCK, NY)) for n in range(NY // CELL_BLOCK)]
    return jnp.concatenate(cells, axis=0).T[:count]


def stay(*arrays):
    return [pltpu.with_memory_space_constraint(x, pltpu.HBM) for x in arrays]


def pack_kernel(viscosity_ref, region_ref, start_ref, heat_ref, outer_ref, inner_ref, sems):
    slab = start_ref.shape[0]
    odd = lax.axis_index("space") % 2
    copies = []
    for n, (edge, last) in enumerate(((outer_ref, odd), (inner_ref, 1 - odd))):
        first = pl.multiple_of(last * (slab - HALO), CELL_BLOCK)
        for m, field in enumerate((start_ref, heat_ref)):
            target = edge.at[pl.ds(m * HALO, HALO)]
            copies.append(pltpu.make_async_copy(field.at[pl.ds(first, HALO)], target, sems.at[2 * n + m]))
    for copy in copies:
        copy.start()
    spread = spread_blocks(viscosity_ref, region_ref)
    head, tail = spread[:8], spread[spread.shape[0] - 8 :]
    outer_ref[2 * HALO :, :] = jnp.where(odd == 1, tail, head)
    inner_ref[2 * HALO :, :] = jnp.where(odd == 1, head, tail)
    for copy in copies:
        copy.wait()


def pack(viscosity, region, start, heat):
    edge = (PACK, NY)
    return pl.pallas_call(
        pack_kernel,
        out_shape=(jax.ShapeDtypeStruct(edge, jnp.float32), jax.ShapeDtypeStruct(edge, jnp.float32)),
        in_specs=[pl.BlockSpec(memory_space=pltpu.SMEM), whole(region.shape), ANYWHERE, ANYWHERE],
        out_specs=(whole(edge), whole(edge)),
        scratch_shapes=[pltpu.SemaphoreType.DMA((4,))],
        compiler_params=pltpu.CompilerParams(vmem_limit_bytes=SMALL_VMEM_LIMIT),
        name="pack",
    )(viscosity, region, start, heat)


def stage_kernel(viscosity_ref, region_ref, fine_ref, coarse_ref, fine_rhs, coarse_rhs, base_ref):
    spread = spread_blocks(viscosity_ref, region_ref)
    for b in range(spread.shape[0]):
        base_ref[CELL_BLOCK * b : CELL_BLOCK * (b + 1), :] = jnp.broadcast_to(spread[b : b + 1], (CELL_BLOCK, NY))
    fine_rhs[...] = line_operand(fine_ref)
    coarse_rhs[...] = line_operand(coarse_ref)


def stage(viscosity, region, fine_line, coarse_line):
    rows = region.shape[1] * CELL_BLOCK
    square = (2 * NY, 2 * NY)
    return pl.pallas_call(
        stage_kernel,
        out_shape=(
            jax.ShapeDtypeStruct(square, jnp.bfloat16),
            jax.ShapeDtypeStruct(square, jnp.bfloat16),
            jax.ShapeDtypeStruct((rows, NY), jnp.float32),
        ),
        in_specs=[pl.BlockSpec(memory_space=pltpu.SMEM), whole(region.shape), whole((NY, NY)), whole((NY, NY))],
        out_specs=(whole(square), whole(square), whole((rows, NY))),
        compiler_params=pltpu.CompilerParams(vmem_limit_bytes=SMALL_VMEM_LIMIT),
        cost_estimate=pl.CostEstimate(flops=rows * NY, bytes_accessed=8 * rows * NY, transcendentals=0),
        name="stage",
    )(viscosity, region, fine_line, coarse_line)


def fine_kernel(
    ends,
    outer_ref,
    inner_ref,
    start_ref,
    heat_ref,
    middle_ref,
    fine_rhs,
    coarse_rhs,
    windows_ref,
    own_ref,
    base_ref,
    source_ref,
    base_window_ref,
    source_window_ref,
    plain_u,
    plain_q,
    plain_m,
    u_ref,
    still_ref,
    slope_ref,
    w_ref,
):
    space, group = lax.axis_index("space"), lax.axis_index("tm")
    slab = start_ref.shape[0]
    total = slab + 2 * HALO
    tiles = total // 8
    odd = space % 2 == 1

    def low(rows):
        return jnp.where(odd, inner_ref[rows, :], outer_ref[rows, :])

    def high(rows):
        return jnp.where(odd, outer_ref[rows, :], inner_ref[rows, :])

    for plain, part, middle in ((plain_u, 0, start_ref), (plain_q, HALO, heat_ref)):
        plain[0:HALO, :] = low(slice(part, part + HALO))
        plain[HALO : HALO + slab, :] = middle[...]
        plain[HALO + slab :, :] = high(slice(part, part + HALO))
    plain_m[HALO : HALO + slab, :] = middle_ref[...]
    low_blocks, high_blocks = low(slice(2 * HALO, PACK)), high(slice(2 * HALO, PACK))
    for b in range(HALO_BLOCKS):
        n = 8 - HALO_BLOCKS + b
        rows = slice(CELL_BLOCK * b, CELL_BLOCK * (b + 1))
        plain_m[rows, :] = jnp.broadcast_to(low_blocks[n : n + 1, :], (CELL_BLOCK, NY))
        rows = slice(HALO + slab + CELL_BLOCK * b, HALO + slab + CELL_BLOCK * (b + 1))
        plain_m[rows, :] = jnp.broadcast_to(high_blocks[b : b + 1, :], (CELL_BLOCK, NY))
    parts = windows_ref.shape[0]
    each = slab // parts
    reach = (WINDOW - each) // 2
    second = group >= parts
    place = jnp.where(second, group - parts, group)
    corner = pl.multiple_of(placed(second, place, parts) * each + (HALO - reach), CELL_BLOCK)
    base_window_ref[...] = plain_m[pl.ds(corner, WINDOW), :]
    source_window_ref[...] = plain_q[pl.ds(corner, WINDOW), :]
    for plain, ref in ((plain_u, u_ref), (plain_q, source_ref), (plain_m, base_ref)):
        for t in range(tiles):
            ref[8 * t : 8 * t + 8, :] = plain[pl.ds(t, 8, stride=tiles), :]

    under, over = divmod(HALO - 1, tiles), divmod(HALO + slab, tiles)
    walls = [(under[1], wall(space == 0, under[0])), (over[1], wall(space == ends, over[0]))]
    fields = (u_ref, base_ref, source_ref, still_ref, slope_ref, w_ref)

    def store_own(begin, size, value):
        own_ref[begin : begin + size, :] = value

    def store_u(begin, size, value):
        u_ref[begin : begin + size, :] = value

    advance(tiles, GROUPS_OF_TILES, *fields, coarse_rhs, COARSE_C, COARSE_R, COARSE_Q, walls, store_own)

    def step(_, carry):
        advance(tiles, GROUPS_OF_TILES, *fields, fine_rhs, FINE_C, FINE_R, 1.0, walls, store_u)
        return carry

    lax.fori_loop(0, STEPS, step, 0, unroll=STEPS)
    for t in range(tiles):
        rows = slice(8 * t, 8 * t + 8)
        value = u_ref[rows, :]
        value = jnp.where(group == 0, value, value - own_ref[rows, :])
        own_ref[rows, :] = value
        plain_u[pl.ds(t, 8, stride=tiles), :] = value
    for k in range(parts):
        first = pl.multiple_of(placed(second, k, parts) * each + (HALO - reach), CELL_BLOCK)
        windows_ref[k] = plain_u[pl.ds(first, WINDOW), :]


def fine_phase(parts, ends, outer, inner, start, heat, base, fine_rhs, coarse_rhs):
    total = start.shape[0] + 2 * HALO
    operands = (outer, inner, start, heat, base, fine_rhs, coarse_rhs)
    field = jax.ShapeDtypeStruct((total, NY), jnp.float32)
    window = jax.ShapeDtypeStruct((WINDOW, NY), jnp.float32)
    return pl.pallas_call(
        functools.partial(fine_kernel, ends),
        out_shape=(jax.ShapeDtypeStruct((parts, WINDOW, NY), jnp.float32), field, field, field, window, window),
        in_specs=[whole(x.shape) for x in operands],
        out_specs=(whole((parts, WINDOW, NY)), *[whole(field.shape)] * 3, *[whole(window.shape)] * 2),
        scratch_shapes=[pltpu.VMEM((total, NY), jnp.float32)] * 7,
        compiler_params=pltpu.CompilerParams(vmem_limit_bytes=VMEM_LIMIT),
        name="fine_phase",
    )(*operands)


def sweep_window(ends, jumps_ref, base_window_ref, source_window_ref, rhs, back_ref, begin_ref, first, last, scratch):
    u_ref, base_ref, source_ref, still_ref, slope_ref, w_ref, plain = scratch
    parts = jumps_ref.shape[0]
    space, group = lax.axis_index("space"), lax.axis_index("tm")
    tiles = WINDOW // 8
    for t in range(tiles):
        rows = slice(8 * t, 8 * t + 8)
        u_ref[rows, :] = begin_ref[pl.ds(t, 8, stride=tiles), :]
        base_ref[rows, :] = base_window_ref[pl.ds(t, 8, stride=tiles), :]
        source_ref[rows, :] = source_window_ref[pl.ds(t, 8, stride=tiles), :]
    back_ref[first] = begin_ref[MARGIN : MARGIN + BACK, :]
    side = HALO - CELL_BLOCK
    each = WINDOW - 2 * side
    second = group >= parts
    window = placed(second, jnp.where(second, group - parts, group), parts)
    under, over = divmod(side - 1, tiles), divmod(side + each, tiles)
    walls = [
        (under[1], wall((space == 0) & (window == 0), under[0])),
        (over[1], wall((space == ends) & (window == parts - 1), over[0])),
    ]
    fields = (u_ref, base_ref, source_ref, still_ref, slope_ref, w_ref)

    def turn(g, carry):
        def store(begin, size, value):
            for n in range(size // 8):
                t = begin // 8 + n
                moved = value[8 * n : 8 * n + 8] + jumps_ref[g, pl.ds(t, 8, stride=tiles), :]
                u_ref[8 * t : 8 * t + 8, :] = moved
                plain[pl.ds(t, 8, stride=tiles), :] = moved

        advance(tiles, SWEEP_GROUPS_OF_TILES, *fields, rhs, COARSE_C, COARSE_R, COARSE_Q, walls, store)

        @pl.when(g + 1 < parts)
        def _():
            back_ref[g + 1] = plain[MARGIN : MARGIN + BACK, :]

        return carry

    lax.fori_loop(first, last, turn, 0)


def first_sweep_kernel(ends, jumps_ref, base_window_ref, source_window_ref, rhs, back_ref, over_ref, *scratch):
    parts = jumps_ref.shape[0]

    @pl.when(lax.axis_index("tm") < parts)
    def _():
        back_ref[0] = jnp.zeros((BACK, NY), jnp.float32)
        windows = (jumps_ref, base_window_ref, source_window_ref, rhs)
        sweep_window(ends, *windows, back_ref, jumps_ref.at[0], 1, parts, scratch)
        over_ref[...] = scratch[-1][8 : 8 + OVER, :]


def second_sweep_kernel(ends, jumps_ref, base_window_ref, source_window_ref, rhs, first_ref, over_ref, back_ref, *scratch):
    parts = jumps_ref.shape[0]
    second = lax.axis_index("tm") >= parts

    @pl.when(jnp.logical_not(second))
    def _():
        back_ref[...] = first_ref[...]

    @pl.when(second)
    def _():
        windows = (jumps_ref, base_window_ref, source_window_ref, rhs)
        begin_ref = scratch[-1]
        unused = jnp.zeros((8, NY), jnp.float32)
        begin_ref[0:8, :] = unused
        begin_ref[8 : 8 + OVER, :] = over_ref[...]
        begin_ref[8 + OVER :, :] = unused
        sweep_window(ends, *windows, back_ref, begin_ref, 0, parts - 1, scratch)


def sweep(kernel, ends, outputs, *operands):
    window = pltpu.VMEM((WINDOW, NY), jnp.float32)
    return pl.pallas_call(
        functools.partial(kernel, ends),
        out_shape=tuple(jax.ShapeDtypeStruct(shape, jnp.float32) for shape in outputs),
        in_specs=[whole(x.shape) for x in operands],
        out_specs=tuple(whole(shape) for shape in outputs),
        scratch_shapes=[window] * 7,
        compiler_params=pltpu.CompilerParams(vmem_limit_bytes=VMEM_LIMIT),
        name="sweep",
    )(*operands)


def last_kernel(
    ends, parts_ref, own_ref, base_ref, source_ref, start_ref, rhs, ends_ref, next_ref, plain, u_ref, still_ref, slope_ref, w_ref
):
    space, group = lax.axis_index("space"), lax.axis_index("tm")
    parts = parts_ref.shape[0]
    slab = next_ref.shape[0]
    total = slab + 2 * HALO
    tiles = total // 8
    each = slab // parts
    side = (BACK - each) // 2
    empty = jnp.zeros((HALO - 8, NY), jnp.float32)
    plain[0 : HALO - 8, :] = empty
    plain[total - HALO + 8 :, :] = empty
    gap = jnp.zeros((8 - side, NY), jnp.float32)
    second = group >= parts
    lowest = parts_ref[placed(second, 0, parts), 0:side, :]
    highest = parts_ref[placed(second, parts - 1, parts), BACK - side : BACK, :]
    plain[HALO - 8 : HALO, :] = jnp.concatenate([gap, lowest], axis=0)
    plain[HALO + slab : HALO + slab + 8, :] = jnp.concatenate([highest, gap], axis=0)
    for k in range(parts):
        value = parts_ref[placed(second, k, parts), side : side + each, :]
        plain[HALO + each * k : HALO + each * (k + 1), :] = value
        rows = slice(each * k, each * (k + 1))
        next_ref[rows, :] = jnp.where(group == 0, start_ref[rows, :], value)
    for t in range(tiles):
        u_ref[8 * t : 8 * t + 8, :] = plain[pl.ds(t, 8, stride=tiles), :]
    under, over = divmod(HALO - 1, tiles), divmod(HALO + slab, tiles)
    walls = [(under[1], wall(space == 0, under[0])), (over[1], wall(space == ends, over[0]))]

    def store(begin, size, value):
        for n in range(size // 8):
            t = begin // 8 + n
            own = own_ref[8 * t : 8 * t + 8, :]
            moved = value[8 * n : 8 * n + 8]
            plain[pl.ds(t, 8, stride=tiles), :] = jnp.where(group == 0, own, moved + own)

    fields = (u_ref, base_ref, source_ref, still_ref, slope_ref, w_ref)
    advance(tiles, GROUPS_OF_TILES, *fields, rhs, COARSE_C, COARSE_R, COARSE_Q, walls, store)
    ends_ref[...] = plain[HALO : HALO + slab, :]


def last_step(ends, back, own, base, source, start, coarse_rhs):
    field = jax.ShapeDtypeStruct(start.shape, jnp.float32)
    total = own.shape
    return pl.pallas_call(
        functools.partial(last_kernel, ends),
        out_shape=(field, field),
        in_specs=[whole(back.shape), whole(total), whole(total), whole(total), whole(start.shape), whole(coarse_rhs.shape)],
        out_specs=(whole(start.shape), whole(start.shape)),
        scratch_shapes=[pltpu.VMEM(total, jnp.float32)] * 5,
        compiler_params=pltpu.CompilerParams(vmem_limit_bytes=VMEM_LIMIT),
        name="last_step",
    )(back, own, base, source, start, coarse_rhs)


def on_device(starts, region, viscosity, heat_source, fine_line, coarse_line):
    start = starts[0]
    groups = lax.axis_size("tm")
    parts = groups // BLOCKS
    members = [list(range(parts)), list(range(parts, groups))]
    ends = lax.axis_size("space") - 1
    outer, inner = pack(*stay(viscosity, region.T, start, heat_source))
    apart = [(i, i + 1) for i in range(1, ends, 2)]
    within = [(i, i + 1) for i in range(0, ends, 2)]
    outer, inner = (lax.ppermute(x, "space", pairs + [(j, i) for i, j in pairs]) for x, pairs in ((outer, apart), (inner, within)))
    fine_rhs, coarse_rhs, middle = stage(*stay(viscosity, region.T, fine_line, coarse_line))
    windows, own, base, source, base_window, source_window = fine_phase(
        parts, ends, outer, inner, start, heat_source, middle, fine_rhs, coarse_rhs
    )
    jumps = lax.all_to_all(windows, "tm", 0, 0, axis_index_groups=members)
    back_shape = (parts, BACK, NY)
    given = (jumps, base_window, source_window, coarse_rhs)
    first_back, over = sweep(first_sweep_kernel, ends, (back_shape, (OVER, NY)), *given)
    over = lax.ppermute(over, "tm", [(k, parts + mirrored(k, parts)) for k in range(parts)])
    (back,) = sweep(second_sweep_kernel, ends, (back_shape,), *given, first_back, over)
    mine = lax.all_to_all(back, "tm", 0, 0, axis_index_groups=members)
    value, following = last_step(ends, mine, own, base, source, start, coarse_rhs)
    return value[None], following[None]


def solution(mesh):
    placed = (P("tm", "space", None), P("space", None), P(), P("space", None), P(), P())
    return jax.shard_map(
        on_device,
        mesh=mesh,
        in_specs=placed,
        out_specs=(P("tm", "space", None), P("tm", "space", None)),
        check_vma=False,
    )
```

```python
import functools

import jax
import jax.numpy as jnp
from jax import lax
from jax.experimental import pallas as pl
from jax.experimental.pallas import tpu as pltpu
from jax.sharding import PartitionSpec as P

NY = 128
CELL_BLOCK = 16
REGIONS = 8
STEPS = 8

FINE_C = 0.3
FINE_R = 0.2
COARSE_C = 0.5
COARSE_R = 0.12
COARSE_Q = 3.0

HALO = 48
HALO_BLOCKS = HALO // CELL_BLOCK
PACK = 2 * HALO + 8
WINDOW = 192
MARGIN = 28
BACK = WINDOW - 2 * MARGIN
OVER = WINDOW - 16
BLOCKS = 2
GROUPS_OF_TILES = 6
SWEEP_GROUPS_OF_TILES = 2
VMEM_LIMIT = 16 * 1024 * 1024
SMALL_VMEM_LIMIT = 4 * 1024 * 1024


def from_left(tile):
    return pltpu.roll(tile, 1, 0)


def from_right(tile):
    return pltpu.roll(tile, 7, 0)


def halves(x):
    high = x.astype(jnp.bfloat16)
    low = (x - high.astype(jnp.float32)).astype(jnp.bfloat16)
    return high, low


def line_operand(line_ref):
    high, low = halves(line_ref[...].T)
    top = jnp.concatenate([high, low], axis=1)
    return jnp.concatenate([top, top], axis=0)


def product(pairs, rhs_ref):
    left = jnp.concatenate([jnp.concatenate(halves(e), axis=1) for e in pairs], axis=0)
    both = jnp.dot(left, rhs_ref[...], preferred_element_type=jnp.float32)
    return both[:, :NY] + both[:, NY:]


def rotated(pairs, count, turn):
    cuts = [pairs * n // count for n in range(count + 1)]
    groups = [list(range(cuts[n], cuts[n + 1])) for n in range(count)]
    return groups[turn:] + groups[:turn]


def flux_pass(groups, viscosity_of, slope_of, base_of, walls, rhs_ref, store):
    order = [i for group in groups for i in group]
    pairs = len(order)
    begin, prior = order[0], order[-1]
    m_begin = m = viscosity_of(begin)
    top = m[:8]
    if begin == 0:
        top = from_right(top)
    before = (viscosity_of(prior)[8:] + top) * slope_of(prior)[8:]
    if begin == 0:
        before = from_left(before)
    n = 0
    for group in groups:
        done = []
        for i in group:
            n += 1
            following = m_begin if n == pairs else viscosity_of(order[n])
            top = following[:8]
            if i + 1 == pairs:
                top = from_right(top)
            flux = (m + jnp.concatenate([m[8:], top], axis=0)) * slope_of(i)
            e = base_of(i) + (flux - jnp.concatenate([before, flux[:8]], axis=0))
            for tile, mask in walls:
                if tile // 2 == i:
                    ones = jnp.ones_like(mask)
                    both = [mask, ones] if tile % 2 == 0 else [ones, mask]
                    e = e * jnp.concatenate(both, axis=0)
            before = flux[8:]
            if i + 1 == pairs:
                before = from_left(before)
            m = following
            done.append(e)
        store(16 * group[0], 16 * len(group), product(done, rhs_ref))


def recent(compute, count):
    kept = {}

    def call(i):
        if i in kept:
            kept[i] = kept.pop(i)
        else:
            kept[i] = compute(i)
            if len(kept) > count:
                del kept[next(iter(kept))]
        return kept[i]

    return call


def advance(tiles, parts, u_ref, base_ref, heat_ref, still_ref, slope_ref, w_ref, rhs_ref, courant, ratio, weight, walls, store):
    pairs = tiles // 2

    def rows(i):
        return slice(16 * i, 16 * i + 16)

    u_at = recent(lambda i: u_ref[rows(i), :], 3)

    def viscosity_first(i):
        u = u_at(i)
        return base_ref[rows(i), :] / (2.0 + u * u)

    def viscosity_second(i):
        u = 0.5 * (u_ref[rows(i), :] + w_ref[rows(i), :])
        return base_ref[rows(i), :] / (2.0 + u * u)

    right = from_right(u_ref[0:8, :])

    def step(i):
        u = u_at(i)
        top = u_at(i + 1)[:8] if i + 1 < pairs else right
        return jnp.concatenate([u[8:], top], axis=0) - u

    step_up = recent(step, 2)

    def slope_first(i):
        return ratio * step_up(i)

    def still_first(i):
        up = step_up(i)
        slope_ref[rows(i), :] = ratio * up
        prior = from_left(step_up(pairs - 1)[8:]) if i == 0 else step_up(i - 1)[8:]
        heat = heat_ref[rows(i), :]
        if weight != 1.0:
            heat = weight * heat
        still = (u_at(i) + heat) - courant * jnp.concatenate([prior, up[:8]], axis=0)
        still_ref[rows(i), :] = still
        return still

    def store_first(start, count, value):
        w_ref[start : start + count, :] = value

    flux_pass(rotated(pairs, parts, 0), viscosity_first, slope_first, still_first, walls, rhs_ref, store_first)
    flux_pass(
        rotated(pairs, parts, parts // 2),
        viscosity_second,
        lambda i: slope_ref[rows(i), :],
        lambda i: still_ref[rows(i), :],
        walls,
        rhs_ref,
        store,
    )


def wall(at_wall, sublane):
    row = lax.broadcasted_iota(jnp.int32, (8, NY), 0)
    return jnp.where((row == sublane) & at_wall, 0.0, 1.0)


def mirrored(part, parts):
    return (parts // 2 - 1 - part // 2) * 2 + part % 2


def placed(second, part, parts):
    return jnp.where(second, mirrored(part, parts), part)


def whole(shape):
    return pl.BlockSpec(shape, lambda: (0,) * len(shape))


ANYWHERE = pl.BlockSpec(memory_space=pl.ANY)


def spread_blocks(viscosity_ref, region_ref):
    region = region_ref[...]
    count = region.shape[1]
    picked = jnp.zeros(region.shape, jnp.float32)
    for value in range(REGIONS):
        picked = jnp.where(region == value, viscosity_ref[value], picked)
    wide = jnp.concatenate([picked, jnp.zeros((region.shape[0], NY - count), jnp.float32)], axis=1)
    cells = [jnp.broadcast_to(wide[n : n + 1], (CELL_BLOCK, NY)) for n in range(NY // CELL_BLOCK)]
    return jnp.concatenate(cells, axis=0).T[:count]


def stay(*arrays):
    return [pltpu.with_memory_space_constraint(x, pltpu.HBM) for x in arrays]


def pack_kernel(viscosity_ref, region_ref, start_ref, heat_ref, outer_ref, inner_ref, sems):
    slab = start_ref.shape[0]
    odd = lax.axis_index("space") % 2
    copies = []
    for n, (edge, last) in enumerate(((outer_ref, odd), (inner_ref, 1 - odd))):
        first = pl.multiple_of(last * (slab - HALO), CELL_BLOCK)
        for m, field in enumerate((start_ref, heat_ref)):
            target = edge.at[pl.ds(m * HALO, HALO)]
            copies.append(pltpu.make_async_copy(field.at[pl.ds(first, HALO)], target, sems.at[2 * n + m]))
    for copy in copies:
        copy.start()
    spread = spread_blocks(viscosity_ref, region_ref)
    head, tail = spread[:8], spread[spread.shape[0] - 8 :]
    outer_ref[2 * HALO :, :] = jnp.where(odd == 1, tail, head)
    inner_ref[2 * HALO :, :] = jnp.where(odd == 1, head, tail)
    for copy in copies:
        copy.wait()


def pack(viscosity, region, start, heat):
    edge = (PACK, NY)
    return pl.pallas_call(
        pack_kernel,
        out_shape=(jax.ShapeDtypeStruct(edge, jnp.float32), jax.ShapeDtypeStruct(edge, jnp.float32)),
        in_specs=[pl.BlockSpec(memory_space=pltpu.SMEM), whole(region.shape), ANYWHERE, ANYWHERE],
        out_specs=(whole(edge), whole(edge)),
        scratch_shapes=[pltpu.SemaphoreType.DMA((4,))],
        compiler_params=pltpu.CompilerParams(vmem_limit_bytes=SMALL_VMEM_LIMIT),
        name="pack",
    )(viscosity, region, start, heat)


def stage_kernel(viscosity_ref, region_ref, fine_ref, coarse_ref, fine_rhs, coarse_rhs, base_ref):
    spread = spread_blocks(viscosity_ref, region_ref)
    for b in range(spread.shape[0]):
        base_ref[CELL_BLOCK * b : CELL_BLOCK * (b + 1), :] = jnp.broadcast_to(spread[b : b + 1], (CELL_BLOCK, NY))
    fine_rhs[...] = line_operand(fine_ref)
    coarse_rhs[...] = line_operand(coarse_ref)


def stage(viscosity, region, fine_line, coarse_line):
    rows = region.shape[1] * CELL_BLOCK
    square = (2 * NY, 2 * NY)
    return pl.pallas_call(
        stage_kernel,
        out_shape=(
            jax.ShapeDtypeStruct(square, jnp.bfloat16),
            jax.ShapeDtypeStruct(square, jnp.bfloat16),
            jax.ShapeDtypeStruct((rows, NY), jnp.float32),
        ),
        in_specs=[pl.BlockSpec(memory_space=pltpu.SMEM), whole(region.shape), whole((NY, NY)), whole((NY, NY))],
        out_specs=(whole(square), whole(square), whole((rows, NY))),
        compiler_params=pltpu.CompilerParams(vmem_limit_bytes=SMALL_VMEM_LIMIT),
        cost_estimate=pl.CostEstimate(flops=rows * NY, bytes_accessed=8 * rows * NY, transcendentals=0),
        name="stage",
    )(viscosity, region, fine_line, coarse_line)


def fine_kernel(
    ends,
    outer_ref,
    inner_ref,
    start_ref,
    heat_ref,
    middle_ref,
    fine_rhs,
    coarse_rhs,
    windows_ref,
    own_ref,
    base_ref,
    source_ref,
    base_window_ref,
    source_window_ref,
    plain_u,
    plain_q,
    plain_m,
    u_ref,
    still_ref,
    slope_ref,
    w_ref,
):
    space, group = lax.axis_index("space"), lax.axis_index("tm")
    slab = start_ref.shape[0]
    total = slab + 2 * HALO
    tiles = total // 8
    odd = space % 2 == 1

    def low(rows):
        return jnp.where(odd, inner_ref[rows, :], outer_ref[rows, :])

    def high(rows):
        return jnp.where(odd, outer_ref[rows, :], inner_ref[rows, :])

    for plain, part, middle in ((plain_u, 0, start_ref), (plain_q, HALO, heat_ref)):
        plain[0:HALO, :] = low(slice(part, part + HALO))
        plain[HALO : HALO + slab, :] = middle[...]
        plain[HALO + slab :, :] = high(slice(part, part + HALO))
    plain_m[HALO : HALO + slab, :] = middle_ref[...]
    low_blocks, high_blocks = low(slice(2 * HALO, PACK)), high(slice(2 * HALO, PACK))
    for b in range(HALO_BLOCKS):
        n = 8 - HALO_BLOCKS + b
        rows = slice(CELL_BLOCK * b, CELL_BLOCK * (b + 1))
        plain_m[rows, :] = jnp.broadcast_to(low_blocks[n : n + 1, :], (CELL_BLOCK, NY))
        rows = slice(HALO + slab + CELL_BLOCK * b, HALO + slab + CELL_BLOCK * (b + 1))
        plain_m[rows, :] = jnp.broadcast_to(high_blocks[b : b + 1, :], (CELL_BLOCK, NY))
    parts = windows_ref.shape[0]
    each = slab // parts
    reach = (WINDOW - each) // 2
    second = group >= parts
    place = jnp.where(second, group - parts, group)
    corner = pl.multiple_of(placed(second, place, parts) * each + (HALO - reach), CELL_BLOCK)
    base_window_ref[...] = plain_m[pl.ds(corner, WINDOW), :]
    source_window_ref[...] = plain_q[pl.ds(corner, WINDOW), :]
    for plain, ref in ((plain_u, u_ref), (plain_q, source_ref), (plain_m, base_ref)):
        for t in range(tiles):
            ref[8 * t : 8 * t + 8, :] = plain[pl.ds(t, 8, stride=tiles), :]

    under, over = divmod(HALO - 1, tiles), divmod(HALO + slab, tiles)
    walls = [(under[1], wall(space == 0, under[0])), (over[1], wall(space == ends, over[0]))]
    fields = (u_ref, base_ref, source_ref, still_ref, slope_ref, w_ref)

    def store_own(begin, size, value):
        own_ref[begin : begin + size, :] = value

    def store_u(begin, size, value):
        u_ref[begin : begin + size, :] = value

    advance(tiles, GROUPS_OF_TILES, *fields, coarse_rhs, COARSE_C, COARSE_R, COARSE_Q, walls, store_own)

    def step(_, carry):
        advance(tiles, GROUPS_OF_TILES, *fields, fine_rhs, FINE_C, FINE_R, 1.0, walls, store_u)
        return carry

    lax.fori_loop(0, STEPS, step, 0, unroll=STEPS)
    for t in range(tiles):
        rows = slice(8 * t, 8 * t + 8)
        value = u_ref[rows, :]
        value = jnp.where(group == 0, value, value - own_ref[rows, :])
        own_ref[rows, :] = value
        plain_u[pl.ds(t, 8, stride=tiles), :] = value
    for k in range(parts):
        first = pl.multiple_of(placed(second, k, parts) * each + (HALO - reach), CELL_BLOCK)
        windows_ref[k] = plain_u[pl.ds(first, WINDOW), :]


def fine_phase(parts, ends, outer, inner, start, heat, base, fine_rhs, coarse_rhs):
    total = start.shape[0] + 2 * HALO
    operands = (outer, inner, start, heat, base, fine_rhs, coarse_rhs)
    field = jax.ShapeDtypeStruct((total, NY), jnp.float32)
    window = jax.ShapeDtypeStruct((WINDOW, NY), jnp.float32)
    return pl.pallas_call(
        functools.partial(fine_kernel, ends),
        out_shape=(jax.ShapeDtypeStruct((parts, WINDOW, NY), jnp.float32), field, field, field, window, window),
        in_specs=[whole(x.shape) for x in operands],
        out_specs=(whole((parts, WINDOW, NY)), *[whole(field.shape)] * 3, *[whole(window.shape)] * 2),
        scratch_shapes=[pltpu.VMEM((total, NY), jnp.float32)] * 7,
        compiler_params=pltpu.CompilerParams(vmem_limit_bytes=VMEM_LIMIT),
        name="fine_phase",
    )(*operands)


def sweep_window(ends, jumps_ref, base_window_ref, source_window_ref, rhs, back_ref, begin_ref, first, last, scratch):
    u_ref, base_ref, source_ref, still_ref, slope_ref, w_ref, plain = scratch
    parts = jumps_ref.shape[0]
    space, group = lax.axis_index("space"), lax.axis_index("tm")
    tiles = WINDOW // 8
    for t in range(tiles):
        rows = slice(8 * t, 8 * t + 8)
        u_ref[rows, :] = begin_ref[pl.ds(t, 8, stride=tiles), :]
        base_ref[rows, :] = base_window_ref[pl.ds(t, 8, stride=tiles), :]
        source_ref[rows, :] = source_window_ref[pl.ds(t, 8, stride=tiles), :]
    back_ref[first] = begin_ref[MARGIN : MARGIN + BACK, :]
    side = HALO - CELL_BLOCK
    each = WINDOW - 2 * side
    second = group >= parts
    window = placed(second, jnp.where(second, group - parts, group), parts)
    under, over = divmod(side - 1, tiles), divmod(side + each, tiles)
    walls = [
        (under[1], wall((space == 0) & (window == 0), under[0])),
        (over[1], wall((space == ends) & (window == parts - 1), over[0])),
    ]
    fields = (u_ref, base_ref, source_ref, still_ref, slope_ref, w_ref)

    def turn(g):
        def store(begin, size, value):
            for n in range(size // 8):
                t = begin // 8 + n
                moved = value[8 * n : 8 * n + 8] + jumps_ref[g, pl.ds(t, 8, stride=tiles), :]
                u_ref[8 * t : 8 * t + 8, :] = moved
                plain[pl.ds(t, 8, stride=tiles), :] = moved

        advance(tiles, SWEEP_GROUPS_OF_TILES, *fields, rhs, COARSE_C, COARSE_R, COARSE_Q, walls, store)
        if g + 1 < parts:
            back_ref[g + 1] = plain[MARGIN : MARGIN + BACK, :]

    for g in range(first, last):
        turn(g)


def first_sweep_kernel(ends, jumps_ref, base_window_ref, source_window_ref, rhs, back_ref, over_ref, *scratch):
    parts = jumps_ref.shape[0]

    @pl.when(lax.axis_index("tm") < parts)
    def _():
        back_ref[0] = jnp.zeros((BACK, NY), jnp.float32)
        windows = (jumps_ref, base_window_ref, source_window_ref, rhs)
        sweep_window(ends, *windows, back_ref, jumps_ref.at[0], 1, parts, scratch)
        over_ref[...] = scratch[-1][8 : 8 + OVER, :]


def second_sweep_kernel(ends, jumps_ref, base_window_ref, source_window_ref, rhs, first_ref, over_ref, back_ref, *scratch):
    parts = jumps_ref.shape[0]
    second = lax.axis_index("tm") >= parts

    @pl.when(jnp.logical_not(second))
    def _():
        back_ref[...] = first_ref[...]

    @pl.when(second)
    def _():
        windows = (jumps_ref, base_window_ref, source_window_ref, rhs)
        begin_ref = scratch[-1]
        unused = jnp.zeros((8, NY), jnp.float32)
        begin_ref[0:8, :] = unused
        begin_ref[8 : 8 + OVER, :] = over_ref[...]
        begin_ref[8 + OVER :, :] = unused
        sweep_window(ends, *windows, back_ref, begin_ref, 0, parts - 1, scratch)


def sweep(kernel, ends, outputs, *operands):
    window = pltpu.VMEM((WINDOW, NY), jnp.float32)
    return pl.pallas_call(
        functools.partial(kernel, ends),
        out_shape=tuple(jax.ShapeDtypeStruct(shape, jnp.float32) for shape in outputs),
        in_specs=[whole(x.shape) for x in operands],
        out_specs=tuple(whole(shape) for shape in outputs),
        scratch_shapes=[window] * 7,
        compiler_params=pltpu.CompilerParams(vmem_limit_bytes=VMEM_LIMIT),
        name="sweep",
    )(*operands)


def last_kernel(
    ends, parts_ref, own_ref, base_ref, source_ref, start_ref, rhs, ends_ref, next_ref, plain, u_ref, still_ref, slope_ref, w_ref
):
    space, group = lax.axis_index("space"), lax.axis_index("tm")
    parts = parts_ref.shape[0]
    slab = next_ref.shape[0]
    total = slab + 2 * HALO
    tiles = total // 8
    each = slab // parts
    side = (BACK - each) // 2
    empty = jnp.zeros((HALO - 8, NY), jnp.float32)
    plain[0 : HALO - 8, :] = empty
    plain[total - HALO + 8 :, :] = empty
    gap = jnp.zeros((8 - side, NY), jnp.float32)
    second = group >= parts
    lowest = parts_ref[placed(second, 0, parts), 0:side, :]
    highest = parts_ref[placed(second, parts - 1, parts), BACK - side : BACK, :]
    plain[HALO - 8 : HALO, :] = jnp.concatenate([gap, lowest], axis=0)
    plain[HALO + slab : HALO + slab + 8, :] = jnp.concatenate([highest, gap], axis=0)
    for k in range(parts):
        value = parts_ref[placed(second, k, parts), side : side + each, :]
        plain[HALO + each * k : HALO + each * (k + 1), :] = value
        rows = slice(each * k, each * (k + 1))
        next_ref[rows, :] = jnp.where(group == 0, start_ref[rows, :], value)
    for t in range(tiles):
        u_ref[8 * t : 8 * t + 8, :] = plain[pl.ds(t, 8, stride=tiles), :]
    under, over = divmod(HALO - 1, tiles), divmod(HALO + slab, tiles)
    walls = [(under[1], wall(space == 0, under[0])), (over[1], wall(space == ends, over[0]))]

    def store(begin, size, value):
        for n in range(size // 8):
            t = begin // 8 + n
            own = own_ref[8 * t : 8 * t + 8, :]
            moved = value[8 * n : 8 * n + 8]
            plain[pl.ds(t, 8, stride=tiles), :] = jnp.where(group == 0, own, moved + own)

    fields = (u_ref, base_ref, source_ref, still_ref, slope_ref, w_ref)
    advance(tiles, GROUPS_OF_TILES, *fields, rhs, COARSE_C, COARSE_R, COARSE_Q, walls, store)
    ends_ref[...] = plain[HALO : HALO + slab, :]


def last_step(ends, back, own, base, source, start, coarse_rhs):
    field = jax.ShapeDtypeStruct(start.shape, jnp.float32)
    total = own.shape
    return pl.pallas_call(
        functools.partial(last_kernel, ends),
        out_shape=(field, field),
        in_specs=[whole(back.shape), whole(total), whole(total), whole(total), whole(start.shape), whole(coarse_rhs.shape)],
        out_specs=(whole(start.shape), whole(start.shape)),
        scratch_shapes=[pltpu.VMEM(total, jnp.float32)] * 5,
        compiler_params=pltpu.CompilerParams(vmem_limit_bytes=VMEM_LIMIT),
        name="last_step",
    )(back, own, base, source, start, coarse_rhs)


def on_device(starts, region, viscosity, heat_source, fine_line, coarse_line):
    start = starts[0]
    groups = lax.axis_size("tm")
    parts = groups // BLOCKS
    members = [list(range(parts)), list(range(parts, groups))]
    ends = lax.axis_size("space") - 1
    outer, inner = pack(*stay(viscosity, region.T, start, heat_source))
    apart = [(i, i + 1) for i in range(1, ends, 2)]
    within = [(i, i + 1) for i in range(0, ends, 2)]
    outer, inner = (lax.ppermute(x, "space", pairs + [(j, i) for i, j in pairs]) for x, pairs in ((outer, apart), (inner, within)))
    fine_rhs, coarse_rhs, middle = stage(*stay(viscosity, region.T, fine_line, coarse_line))
    windows, own, base, source, base_window, source_window = fine_phase(
        parts, ends, outer, inner, start, heat_source, middle, fine_rhs, coarse_rhs
    )
    jumps = lax.all_to_all(windows, "tm", 0, 0, axis_index_groups=members)
    back_shape = (parts, BACK, NY)
    given = (jumps, base_window, source_window, coarse_rhs)
    first_back, over = sweep(first_sweep_kernel, ends, (back_shape, (OVER, NY)), *given)
    over = lax.ppermute(over, "tm", [(k, parts + mirrored(k, parts)) for k in range(parts)])
    (back,) = sweep(second_sweep_kernel, ends, (back_shape,), *given, first_back, over)
    mine = lax.all_to_all(back, "tm", 0, 0, axis_index_groups=members)
    value, following = last_step(ends, mine, own, base, source, start, coarse_rhs)
    return value[None], following[None]


def solution(mesh):
    placed = (P("tm", "space", None), P("space", None), P(), P("space", None), P(), P())
    return jax.shard_map(
        on_device,
        mesh=mesh,
        in_specs=placed,
        out_specs=(P("tm", "space", None), P("tm", "space", None)),
        check_vma=False,
    )
```
